256 devices in a mesh: section: 16 (over y_hi, z), fsdp: 16 (over y_lo, x, core).
Axes of the slice: x: 4, y: 4 (y_hi: 2, y_lo: 2; y = y_hi * 2 + y_lo), z: 8, core: 2. Of those that a mesh axis runs over, the one named last changes fastest.
Arguments:
- patch_rows: bfloat16 [16, 2048, 1280], P('section', 'fsdp'), may hold values from -6 to 6
- query: bfloat16 [16, 2048, 640], P('section', 'fsdp'), may hold values from -32 to 32
- key_rows: bfloat16 [16, 2048, 640], P('section', 'fsdp'), may hold values from -32 to 32
- value_rows: bfloat16 [16, 2048, 640], P('section', 'fsdp'), may hold values from -6 to 6
- image_lengths: int32 [16, 4], P('section'), may hold values from 1 to 256, 512 in all within a row
- token_slots: int32 [16, 512], P('section', 'fsdp'), may hold values from 0 to 2047, as said below
- out_proj: bfloat16 [640, 1280], P('fsdp'), may hold values from -0.25 to 0.25
- merge_gain: float32 [1280], replicated, may hold values from 0.1 to 1.9
- merger_weight: bfloat16 [5120, 4096], P('section', 'fsdp'), may hold values from -0.078125 to 0.078125
- text_rows: bfloat16 [16, 2048, 4096], P('section', 'fsdp'), may hold values from -6 to 6
- norm_gain: float32 [4096], replicated, may hold values from 0.1 to 1.9
- out_grad: bfloat16 [16, 2048, 4096], P('section', 'fsdp'), may hold values from -6 to 6
Outputs:
- llm_input: bfloat16 [16, 2048, 4096], P('section', 'fsdp')
- grad_patches: bfloat16 [16, 2048, 1280], P('section', 'fsdp')
- grad_query: bfloat16 [16, 2048, 640], P('section', 'fsdp')
- grad_key: bfloat16 [16, 2048, 640], P('section', 'fsdp')
- grad_value: bfloat16 [16, 2048, 640], P('section', 'fsdp')
- grad_norm_gain: float32 [4096], replicated
- grad_merge_gain: float32 [1280], replicated
- grad_merger: float32 [5120, 4096], P('section', 'fsdp')
- grad_out_proj: float32 [640, 1280], P('fsdp')
The draws below stay inside these ranges and needn't reach their ends.
Inputs may be any that keep to these rules, and one draw needn't show every extreme that they name: `token_slots`: within a micro-batch the values are distinct, and every block of 128 consecutive token rows receives exactly 32 of them.
All inputs are finite; a program needn't handle non-finite values.
Results may differ from the reference program's by a relative error of at most 0.03.
Values may be sent and summed in bfloat16 or wider, within the bound.
No kernel may reach another device: no remote copies, remote signals or barrier semaphores. Data moves between devices by JAX's collectives and lax.ppermute only.
A program may use at most 128 MiB of HBM per device.

```python
import math
import jax
import jax.numpy as jnp
import numpy as np
from jax import lax

D_VIT = 1280
HEADS = 8
HEAD_DIM = 80
D_LLM = 4096
PATCH_DEV = 128
IMAGES = 4
ATT_W = 640
MERGED_DEV = 32
TOK_DEV = 128
MICRO = 16
PATCHES = 2048
MERGED = 512
TOKENS = 2048
MERGED_W = 5120
N_FSDP = 16


def drawn_pair(key):
    shape = (MICRO, PATCHES, ATT_W)
    base_query = jnp.clip(jax.random.normal(jax.random.fold_in(key, 11), shape, jnp.float32), -6.0, 6.0)
    base_key = jnp.clip(jax.random.normal(jax.random.fold_in(key, 12), shape, jnp.float32), -6.0, 6.0)
    return (base_query, base_key)


def draw_query(key, part):
    return drawn_pair(key)[0].astype(jnp.bfloat16)


def draw_key_rows(key, part):
    return drawn_pair(key)[1].astype(jnp.bfloat16)


def draw_token_slots(key, part):
    owners = TOKENS // TOK_DEV
    owner_keys = jax.random.split(jax.random.fold_in(key, 21), MICRO * owners)
    picks = jax.vmap(lambda single: jax.random.permutation(single, TOK_DEV)[:MERGED_DEV])(owner_keys)
    offsets = jnp.arange(owners, dtype=jnp.int32) * TOK_DEV
    picks = picks.astype(jnp.int32).reshape(MICRO, owners, MERGED_DEV) + offsets[None, :, None]
    picks = picks.reshape(MICRO, MERGED)
    shuffle_keys = jax.random.split(jax.random.fold_in(key, 22), MICRO)
    order = jax.vmap(lambda single: jax.random.permutation(single, MERGED))(shuffle_keys)
    return jnp.take_along_axis(picks, order.astype(jnp.int32), axis=1).astype(jnp.int32)


def level_of(rng, shape, pieces, low, largest):
    def one(position, blocks):
        steps = jax.random.uniform(jax.random.fold_in(jax.random.fold_in(rng, 6), position), (blocks,), jnp.float32, low / len(pieces), largest / len(pieces))
        return jnp.repeat(jnp.exp(steps), shape[position] // blocks).reshape((-1,) + (1,) * (len(shape) - position - 1))

    loudness = one(*pieces[0])
    for cut in pieces[1:]:
        loudness = loudness * one(*cut)
    return loudness


def split_up(count, total, limit, lean):
    weights = [(1 << 20) // math.isqrt(grade ** lean) + 1 for grade in range(2, count + 1)]
    spare, given = total - limit - (count - 1), [1] * (count - 1)
    while spare > 0:
        free = [i for i in range(count - 1) if given[i] < limit]
        pool, left = sum([weights[i] for i in free]), spare
        for i in free:
            addition = min(limit - given[i], max(1, left * weights[i] // pool), spare)
            given[i] = given[i] + addition
            spare = spare - addition
    return np.array([limit] + given)


def uneven_parts(rng, count, total, limit, slope):
    if count == 2:
        one = jax.random.randint(rng, (), max(1, total - limit), min(limit, total - 1) + 1)
        return jnp.stack([one, total - one])
    sizes = jnp.asarray(split_up(count, total, limit, slope), jnp.int32)
    pairs = (count - 1) // 2
    donor, sink = sizes[1:1 + 2 * pairs:2], sizes[2:2 + 2 * pairs:2]
    margin = jnp.minimum(donor - 1, limit - sink)
    moved = jax.random.randint(jax.random.fold_in(rng, 1), (pairs,), 0, 1 << 20) % (margin + 1)
    sizes = sizes.at[1:1 + 2 * pairs:2].set(donor - moved).at[2:2 + 2 * pairs:2].set(sink + moved)
    return sizes[jax.random.permutation(jax.random.fold_in(rng, 2), count)]


def normal_values(stream_key, extent, width, reach, cuts=(), held_as=jnp.bfloat16):
    loudness = level_of(stream_key, extent, cuts, -0.22, 0.18) if cuts else 1.0
    entries = jax.random.normal(stream_key, extent, jnp.float32) * width * loudness
    return jnp.minimum(jnp.maximum(entries, -reach), reach).astype(held_as)


def setup_inputs(seed: int = 0) -> dict:
    key_of = jax.random.split(jax.random.key(seed), 13)
    patch_rows = normal_values(key_of[0], (MICRO, PATCHES, D_VIT), 1.0, 6.0, ((0, 16), (1, 16)))
    query = draw_query(jax.random.fold_in(key_of[12], 71), 0)
    key_rows = draw_key_rows(jax.random.fold_in(key_of[12], 71), 0)
    value_rows = normal_values(key_of[3], (MICRO, PATCHES, ATT_W), 1.0, 6.0, ((0, 16), (1, 16)))
    image_lengths = jax.vmap(lambda own: uneven_parts(own, IMAGES, MERGED, MERGED // 2, 2))(jax.random.split(key_of[4], MICRO)).reshape((MICRO, IMAGES)).astype(jnp.int32)
    token_slots = draw_token_slots(jax.random.fold_in(key_of[12], 71), 0)
    out_proj = normal_values(key_of[6], (ATT_W, D_VIT), ATT_W ** -0.5, 0.25, ((0, 16),))
    merge_gain = jnp.clip(1.0 + 0.18 * jax.random.normal(key_of[7], (D_VIT,), jnp.float32), 0.1, 1.9)
    merger_weight = normal_values(key_of[8], (MERGED_W, D_LLM), MERGED_W ** -0.5, 0.078125, ((0, 16), (1, 16)))
    text_rows = normal_values(key_of[9], (MICRO, TOKENS, D_LLM), 1.0, 6.0, ((0, 16), (1, 16)))
    norm_gain = jnp.clip(1.0 + 0.18 * jax.random.normal(key_of[10], (D_LLM,), jnp.float32), 0.1, 1.9)
    out_grad = normal_values(key_of[11], (MICRO, TOKENS, D_LLM), 1.0, 6.0, ((0, 16), (1, 16)))
    return {"patch_rows": patch_rows, "query": query, "key_rows": key_rows, "value_rows": value_rows, "image_lengths": image_lengths, "token_slots": token_slots, "out_proj": out_proj, "merge_gain": merge_gain, "merger_weight": merger_weight, "text_rows": text_rows, "norm_gain": norm_gain, "out_grad": out_grad}


EPS = 1e-06

def image_ids(lengths, index):
    ends = jnp.cumsum(lengths).astype(jnp.int32)
    merged_index = index // 4
    return lax.optimization_barrier(jnp.sum((merged_index[:, None] >= ends[None, :]).astype(jnp.int32), axis=1))

def head_probs(query_head, key_head, mask):
    scale = query_head.shape[-1] ** (-0.5)
    scores = jnp.dot(query_head, key_head.T, preferred_element_type=jnp.float32) * scale
    scores = jnp.where(mask, scores, -jnp.inf)
    top = lax.optimization_barrier(jnp.max(scores, axis=-1, keepdims=True))
    weights = jnp.where(mask, jnp.exp(scores - top), 0.0)
    return weights / lax.optimization_barrier(jnp.sum(weights, axis=-1, keepdims=True))

def split_heads(rows):
    return rows.reshape(rows.shape[0], HEADS, HEAD_DIM).transpose(1, 0, 2)

def join_heads(heads):
    return heads.transpose(1, 0, 2).reshape(heads.shape[1], HEADS * HEAD_DIM)

def rounded(value):
    low = lax.optimization_barrier(value.astype(jnp.bfloat16))
    return low.astype(jnp.float32)

def blocked_sum(left, right):
    terms = jnp.einsum('fqk,fqd->fkd', left.reshape(N_FSDP, PATCH_DEV, -1).astype(jnp.float32), right.reshape(N_FSDP, PATCH_DEV, -1).astype(jnp.float32), precision=lax.Precision.HIGHEST)
    return lax.optimization_barrier(jnp.sum(rounded(terms), axis=0))

def reference(patch_rows, query, key_rows, value_rows, image_lengths, token_slots, out_proj, merge_gain, merger_weight, text_rows, norm_gain, out_grad):

    def one_micro(carry, inputs):
        patches, queries, keys, values, lengths, slots, text, cotangent = inputs
        count = patches.shape[0]
        ids = image_ids(lengths, jnp.arange(count, dtype=jnp.int32))
        mask = ids[:, None] == ids[None, :]
        query_heads = split_heads(queries)
        key_heads = split_heads(keys)
        value_heads = split_heads(values)

        def forward_head(items):
            probs = head_probs(items[0], items[1], mask)
            return jnp.dot(probs.astype(jnp.bfloat16), items[2], preferred_element_type=jnp.float32)
        attended = join_heads(lax.map(forward_head, (query_heads, key_heads, value_heads))).astype(jnp.bfloat16)
        mixed = patches.astype(jnp.float32) + jnp.dot(attended, out_proj, preferred_element_type=jnp.float32)
        centre = mixed - lax.optimization_barrier(jnp.mean(mixed, axis=-1, keepdims=True))
        inv_std = lax.rsqrt(lax.optimization_barrier(jnp.mean(centre * centre, axis=-1, keepdims=True)) + EPS)
        unit = centre * inv_std
        normed = (unit * merge_gain).astype(jnp.bfloat16)
        merged = normed.reshape(MERGED, MERGED_W)
        projected = jnp.dot(merged, merger_weight, preferred_element_type=jnp.float32).astype(jnp.bfloat16)
        stream = text.at[slots].set(projected).astype(jnp.float32)
        inv_rms = lax.rsqrt(lax.optimization_barrier(jnp.mean(stream * stream, axis=-1, keepdims=True)) + EPS)
        scaled = stream * inv_rms
        llm_input = (scaled * norm_gain).astype(jnp.bfloat16)
        upstream_raw = cotangent.astype(jnp.float32)
        norm_gain_part = lax.optimization_barrier(jnp.sum(upstream_raw * scaled, axis=0))
        upstream = upstream_raw * norm_gain
        stream_grad = inv_rms * (upstream - scaled * lax.optimization_barrier(jnp.mean(upstream * scaled, axis=-1, keepdims=True)))
        image_grad = stream_grad[slots].astype(jnp.bfloat16)
        merger_part = rounded(jnp.dot(merged.T, image_grad, preferred_element_type=jnp.float32))
        columns = D_LLM // N_FSDP
        block_terms = jnp.einsum('mfc,kfc->fmk', image_grad.reshape(MERGED, N_FSDP, columns).astype(jnp.float32), merger_weight.reshape(MERGED_W, N_FSDP, columns).astype(jnp.float32), precision=lax.Precision.HIGHEST)
        merged_grad = lax.optimization_barrier(jnp.sum(rounded(block_terms), axis=0))
        normed_grad = merged_grad.reshape(count, D_VIT)
        merge_gain_part = lax.optimization_barrier(jnp.sum(normed_grad * unit, axis=0))
        unit_grad = normed_grad * merge_gain
        mixed_grad = inv_std * (unit_grad - lax.optimization_barrier(jnp.mean(unit_grad, axis=-1, keepdims=True)) - unit * lax.optimization_barrier(jnp.mean(unit_grad * unit, axis=-1, keepdims=True)))
        mixed_low = mixed_grad.astype(jnp.bfloat16)
        proj_terms = jnp.einsum('fpa,fpb->fab', attended.reshape(N_FSDP, PATCH_DEV, ATT_W).astype(jnp.float32), mixed_low.reshape(N_FSDP, PATCH_DEV, D_VIT).astype(jnp.float32), precision=lax.Precision.HIGHEST)
        proj_part = lax.optimization_barrier(jnp.sum(rounded(proj_terms), axis=0))
        attended_grad = jnp.dot(mixed_low, out_proj.T, preferred_element_type=jnp.float32).astype(jnp.bfloat16)

        def backward_head(items):
            query_head, key_head, value_head, grad_head = items
            scale = query_head.shape[-1] ** (-0.5)
            probs = head_probs(query_head, key_head, mask)
            probs_low = probs.astype(jnp.bfloat16)
            value_grad = blocked_sum(probs_low, grad_head)
            prob_grad = jnp.dot(grad_head, value_head.T, preferred_element_type=jnp.float32)
            score_grad = probs * (prob_grad - lax.optimization_barrier(jnp.sum(prob_grad * probs, axis=-1, keepdims=True)))
            score_low = (score_grad * scale).astype(jnp.bfloat16)
            query_grad = jnp.dot(score_low, key_head, preferred_element_type=jnp.float32)
            key_grad = blocked_sum(score_low, query_head)
            return (query_grad, key_grad, value_grad)
        query_grad, key_grad, value_grad = lax.map(backward_head, (query_heads, key_heads, value_heads, split_heads(attended_grad)))
        outputs = (llm_input, mixed_low, join_heads(query_grad).astype(jnp.bfloat16), join_heads(key_grad).astype(jnp.bfloat16), join_heads(value_grad).astype(jnp.bfloat16))
        carry = (carry[0] + norm_gain_part, carry[1] + merge_gain_part, carry[2] + merger_part, carry[3] + proj_part)
        return (carry, outputs)
    start = (jnp.zeros((D_LLM,), jnp.float32), jnp.zeros((D_VIT,), jnp.float32), jnp.zeros((MERGED_W, D_LLM), jnp.float32), jnp.zeros((ATT_W, D_VIT), jnp.float32))
    totals, outputs = lax.scan(one_micro, start, (patch_rows, query, key_rows, value_rows, image_lengths, token_slots, text_rows, out_grad))
    return (outputs[0], outputs[1], outputs[2], outputs[3], outputs[4], totals[0], totals[1], totals[2], totals[3])
```

```python
import jax
import jax.numpy as jnp
from jax import lax
from jax.experimental import pallas as pl
from jax.experimental.pallas import tpu as pltpu
from jax.sharding import Mesh
from jax.sharding import PartitionSpec as P


HEAD_DIM = 80
FSDP = ("fsdp_0", "fsdp_1", "fsdp_2")
CHIPS = ("fsdp_0", "fsdp_1")
CORE = "fsdp_2"
SECTION = ("section_0", "section_1")
EVERY = SECTION + FSDP
EPS = 1e-06
LOG2E = 1.4426950408889634
SCALE = HEAD_DIM**-0.5
BF = jnp.bfloat16
F32 = jnp.float32


def dotf(a, b, dims):
    return lax.dot_general(a, b, (dims, ((), ())), preferred_element_type=F32)


def exchanged(x, axis):
    return lax.all_to_all(x, axis, split_axis=0, concat_axis=0, tiled=True)


def to_all(x, axis):
    return exchanged(jnp.broadcast_to(x, (lax.axis_size(axis), *x.shape)), axis)


def other_core(x):
    return lax.ppermute(x, CORE, [(0, 1), (1, 0)])


def other_x(x):
    return lax.ppermute(x, "fsdp_1", [(0, 1), (1, 0), (2, 3), (3, 2)])


def shifted(x, axis, by):
    n = lax.axis_size(axis)
    return lax.ppermute(x, axis, [(i, (i + by) % n) for i in range(n)])


def flipped(x, axis, bit):
    return lax.ppermute(x, axis, [(i, i ^ bit) for i in range(lax.axis_size(axis))])


def swapped(x, flip=0):
    pairs = []
    for i in range(256):
        core, low_x, high_x, y = i % 2, i // 2 % 2, i // 4 % 2, i // 8 % 2
        r, q, top = i // 16 % 4, i // 64 % 2, i // 128
        target = ((((y * 2 + high_x) * 4 + r) * 2 + top) * 2 + q) * 4 + low_x * 2 + core
        pairs.append((i, target ^ (flip * 128)))
    return lax.ppermute(x, EVERY, pairs)


def swapped_back(x, flip=0):
    pairs = []
    for i in range(256):
        j = i ^ (flip * 128)
        core, low_x, high_x, y = j % 2, j // 2 % 2, j // 4 % 2, j // 8 % 2
        r, q, top = j // 16 % 4, j // 64 % 2, j // 128
        target = ((((y * 2 + high_x) * 4 + r) * 2 + top) * 2 + q) * 4 + low_x * 2 + core
        pairs.append((i, target))
    return lax.ppermute(x, EVERY, pairs)


def up(x):
    return shifted(x, "section_1", 1)


def down(x):
    return shifted(x, "section_1", -1)


def weight_blocks(block):
    near = swapped(block)
    other = swapped(block, 1)
    at0 = jnp.stack([near, other])
    below1 = up(at0)
    above1 = down(at0)
    below2 = up(below1)
    above2 = down(above1)
    below3 = up(below2)
    above3 = down(above2)
    far0 = up(below3[0])
    far1 = down(above3[1])
    return at0, above1, above2, above3, far0, far1, below3, below2, below1


def weight_kernel(place_ref, *refs):
    blocks, out_ref = refs[:-1], refs[-1]
    top, z = place_ref[0], place_ref[1]

    def put(block, far, other):
        to = (z + far) % 8
        n = (top ^ other) * 2 + to // 4
        rows = pl.ds(pl.multiple_of(to % 4 * 320, 320), 320)
        out_ref[rows, pl.ds(pl.multiple_of(n * 256, 256), 256)] = block

    at0, above1, above2, above3, far0, far1, below3, below2, below1 = blocks
    for far, ref in ((0, at0), (1, above1), (2, above2), (3, above3), (5, below3), (6, below2), (7, below1)):
        put(ref[0], far, 0)
        put(ref[1], far, 1)
    put(far0[...], 4, 0)
    put(far1[...], 4, 1)


def gathered_weight(block, place):
    blocks = weight_blocks(block)
    vmem = pl.BlockSpec(memory_space=pltpu.VMEM)
    return pl.pallas_call(
        weight_kernel,
        in_specs=[pl.BlockSpec(memory_space=pltpu.SMEM)] + [vmem] * 9,
        out_specs=vmem,
        out_shape=jax.ShapeDtypeStruct((1280, 1024), BF),
        cost_estimate=pl.CostEstimate(flops=0, bytes_accessed=5242880, transcendentals=0),
        name="weight",
    )(place, *blocks)


def section_sum(chunks, z, top):
    def chunk(far):
        return lax.dynamic_index_in_dim(chunks, (z + far) % 8, keepdims=False)

    def plus(a, b):
        return (a.astype(F32) + b.astype(F32)).astype(BF)

    far = chunk(4)
    rise = up(far[0])
    fall = down(far[1])
    mine = chunk(3)
    rise = jnp.stack([plus(mine[0], rise), mine[1]])
    mine = chunk(5)
    fall = jnp.stack([mine[0], plus(mine[1], fall)])
    for step in (2, 3, 4):
        rise = up(rise)
        fall = down(fall)
        if step < 4:
            rise, fall = plus(chunk(4 - step), rise), plus(chunk(4 + step), fall)
    total = chunk(0).astype(F32) + rise.astype(F32) + fall.astype(F32)
    total = total.astype(BF)
    near = lax.dynamic_index_in_dim(total, top, keepdims=False)
    other = lax.dynamic_index_in_dim(total, 1 - top, keepdims=False)
    return swapped_back(near).astype(F32) + swapped_back(other, 1).astype(F32)


def all_sum(x, steps):
    for axis, bit in steps:
        x = (x.astype(F32) + flipped(x, axis, bit).astype(F32)).astype(x.dtype)
    return x


IN_SECTION = (("section_1", 1), ("section_1", 2), ("section_1", 4), ("section_0", 1))


def by_patch(dtype, shape=(128, 128)):
    row = lax.broadcasted_iota(jnp.int32, shape, 0)
    col = lax.broadcasted_iota(jnp.int32, shape, 1)
    return (col == 4 * (row % 32) + row // 32).astype(dtype)


def pack_kernel(q_ref, k_ref, v_ref, x_ref, slot_ref, proj_ref, out_ref, rows_ref):
    order = by_patch(BF)
    q = dotf(order, q_ref[...], ((1,), (0,)))
    k = k_ref[...].astype(F32)
    v = v_ref[...].astype(F32)
    slots = slot_ref[...]
    high = (slots // 128).astype(F32)
    low = (slots % 128).astype(F32)
    column = lax.broadcasted_iota(jnp.int32, (128, 16), 1)
    extra = jnp.where(column == 0, high, jnp.where(column == 1, low, 0.0))
    for h in range(8):
        at = slice(h * HEAD_DIM, (h + 1) * HEAD_DIM)
        out_ref[h] = jnp.concatenate([k[:, at], v[:, at], q[:, at], extra], axis=1).astype(BF)
    x = dotf(order, x_ref[...], ((1,), (0,))).astype(BF)
    for a in range(4):
        for j in range(2):
            rows_ref[2 * a + j, 0:32] = x[a * 32 : (a + 1) * 32]
            rows_ref[2 * a + j, 32:72] = proj_ref[...]


def packed(q, k, v, x, slots, proj):
    return pl.pallas_call(
        pack_kernel,
        out_shape=(
            jax.ShapeDtypeStruct((8, 128, 256), BF),
            jax.ShapeDtypeStruct((8, 72, 1280), BF),
        ),
        name="pack",
    )(q, k, v, x, slots, proj)


def halves(x):
    high = x.astype(BF).astype(F32)
    return high, x - high


def merge_kernel(keep_ref, add_ref, gain_ref, out_ref):
    high, low = halves(gain_ref[...])
    gains = jnp.concatenate([high, low], axis=0).T
    for g in range(8):
        both = keep_ref[g].astype(F32) + add_ref[g].astype(F32)
        out_ref[g] = jnp.concatenate([both[:, 0:240], gains], axis=1).astype(BF)


def merged_grads(keep, add, gains):
    return pl.pallas_call(merge_kernel, out_shape=jax.ShapeDtypeStruct((8, 128, 256), BF), name="merge")(keep, add, gains)


def unpack_kernel(in_ref, msg_ref, p_ref, q_ref, k_ref, v_ref, norm_ref, merge_ref):
    k_ref[...] = jnp.concatenate([in_ref[h][:, 0:80].astype(F32) for h in range(8)], axis=1).astype(BF)
    v_ref[...] = jnp.concatenate([in_ref[h][:, 80:160].astype(F32) for h in range(8)], axis=1).astype(BF)
    q = jnp.concatenate([in_ref[h][:, 160:240].astype(F32) for h in range(8)], axis=1).astype(BF)
    order = by_patch(BF)
    q_ref[...] = dotf(order, q, ((0,), (0,))).astype(BF)
    for j in range(10):
        g = jnp.concatenate([msg_ref[h, 80 + 16 * j : 96 + 16 * j] for h in range(8)], axis=0)
        p_ref[:, j * 128 : (j + 1) * 128] = dotf(order, g, ((0,), (0,))).astype(BF)
    merge_ref[...] = jnp.zeros_like(merge_ref)
    for g in range(8):
        both = in_ref[g][:, 240:256].astype(F32).T
        rows = both[0:8] + both[8:16]
        norm_ref[4 * g : 4 * g + 4] = rows[0:4]
        if g < 5:
            merge_ref[2 * g : 2 * g + 2] = rows[4:6]


def unpacked(x, msg):
    one = jax.ShapeDtypeStruct((128, 640), BF)
    return pl.pallas_call(
        unpack_kernel,
        out_shape=(
            jax.ShapeDtypeStruct((128, 1280), BF),
            one,
            one,
            one,
            jax.ShapeDtypeStruct((32, 128), F32),
            jax.ShapeDtypeStruct((16, 128), F32),
        ),
        name="unpack",
    )(x, msg)


def project_kernel(
    place_ref, own_ref, oth_ref, rows_own_ref, rows_oth_ref, gain_ref, order_ref, weight_ref,
    normed_ref, part_ref, unit_ref, inv_ref, proj_ref, wide_s, normed_s
):
    first = place_ref[4] == 0
    low_x = place_ref[3] % 2
    for g in range(8):
        mine = rows_own_ref[g, 32:72].astype(F32)
        theirs = rows_oth_ref[g, 32:72].astype(F32)
        wide_s[g * 80 : g * 80 + 40] = jnp.where(first, mine, theirs)
        wide_s[g * 80 + 40 : g * 80 + 80] = jnp.where(first, theirs, mine)
    proj_ref[...] = wide_s[...].astype(BF)
    for half in range(2):
        for core, (att, rows) in enumerate(((own_ref, rows_own_ref), (oth_ref, rows_oth_ref))):
            at = slice(half * 128, (half + 1) * 128)
            x = jnp.concatenate([rows[g, half * 16 : half * 16 + 16] for g in range(8)], axis=0).astype(F32)
            mixed = x + dotf(att[:, at], proj_ref[...], ((0,), (0,)))
            centre = mixed - jnp.mean(mixed, axis=-1, keepdims=True)
            inv = lax.rsqrt(jnp.mean(centre * centre, axis=-1, keepdims=True) + EPS)
            unit = centre * inv
            to = core * 256 + half * 128
            normed_s[to : to + 128] = (unit * gain_ref[...]).astype(BF)
            if core == 0:

                @pl.when(low_x == half)
                def _():
                    unit_ref[...] = unit
                    inv_ref[...] = inv

    for k in range(5):
        at = slice(k * 256, (k + 1) * 256)
        normed_ref[:, at] = dotf(order_ref[...], normed_s[:, at], ((1,), (0,))).astype(BF)
    for n in range(4):
        at = slice(n * 256, (n + 1) * 256)
        part = dotf(normed_ref[...], weight_ref[:, at], ((1,), (0,))).astype(BF)
        for o in range(16):
            part_ref[o, :, at] = part[o * 32 : (o + 1) * 32]


def project(place, own, oth, rows_own, rows_oth, gain, order, weight):
    vmem = pl.BlockSpec(memory_space=pltpu.VMEM)
    return pl.pallas_call(
        project_kernel,
        in_specs=[pl.BlockSpec(memory_space=pltpu.SMEM)] + [vmem] * 7,
        out_specs=(vmem,) * 5,
        out_shape=(
            jax.ShapeDtypeStruct((512, 1280), BF),
            jax.ShapeDtypeStruct((16, 32, 1024), BF),
            jax.ShapeDtypeStruct((128, 1280), F32),
            jax.ShapeDtypeStruct((128, 1), F32),
            jax.ShapeDtypeStruct((640, 1280), BF),
        ),
        scratch_shapes=[pltpu.VMEM((640, 1280), F32), pltpu.VMEM((512, 1280), BF)],
        name="project",
    )(place, own, oth, rows_own, rows_oth, gain, order, weight)


def back_kernel(grads_ref, order_ref, weight_ref, own_ref, oth_ref, g_s):
    for k in range(4):
        at = slice(k * 256, (k + 1) * 256)
        g_s[:, at] = dotf(order_ref[...], grads_ref[:, at], ((0,), (0,))).astype(BF)
    for k in range(5):
        at = slice(k * 256, (k + 1) * 256)
        part = dotf(g_s[...], weight_ref[at], ((1,), (1,))).astype(BF)
        own_ref[:, at] = part[0:256]
        oth_ref[:, at] = part[256:512]


def project_back(grads, order, weight):
    half = jax.ShapeDtypeStruct((256, 1280), BF)
    return pl.pallas_call(
        back_kernel, out_shape=(half, half), scratch_shapes=[pltpu.VMEM((512, 1024), BF)], name="project_back"
    )(grads, order, weight)


def merger_kernel(normed_ref, grads_ref, out_ref):
    for n in range(4):
        part = dotf(normed_ref[...], grads_ref[:, n * 256 : (n + 1) * 256], ((0,), (0,)))
        for r in range(4):
            out_ref[n % 2 * 4 + r, n // 2] = part[r * 320 : (r + 1) * 320].astype(BF)


def merger_blocks(normed, grads):
    return pl.pallas_call(merger_kernel, out_shape=jax.ShapeDtypeStruct((8, 2, 320, 256), BF), name="merger")(normed, grads)


def norm_back_kernel(place_ref, kept_ref, came_ref, unit_ref, inv_ref, gain_ref, part_ref, att_ref, proj_ref, msg_ref, mine_ref, theirs_ref):
    grad = kept_ref[...] + came_ref[...].astype(F32)
    unit = unit_ref[...]
    merge_part = jnp.sum(grad * unit, axis=0, keepdims=True)
    raised = grad * gain_ref[...]
    mean = jnp.mean(raised, axis=-1, keepdims=True)
    mixed = inv_ref[...] * (raised - mean - unit * jnp.mean(raised * unit, axis=-1, keepdims=True))
    low = mixed.astype(BF)
    att_grad = dotf(proj_ref[...], low, ((1,), (1,))).astype(BF)
    norm_part = part_ref[...]
    none = jnp.zeros((1, 128), F32)
    for g in range(8):
        msg_ref[g, 0:80] = att_grad[g * 80 : (g + 1) * 80]
        for j in range(10):
            msg_ref[g, 80 + 16 * j : 96 + 16 * j] = low[g * 16 : (g + 1) * 16, j * 128 : (j + 1) * 128]
        rows = [norm_part[:, (4 * g + j) * 128 : (4 * g + j + 1) * 128] for j in range(4)]
        rows += [merge_part[:, (2 * g + j) * 128 : (2 * g + j + 1) * 128] if g < 5 else none for j in range(2)]
        high, rest = halves(jnp.concatenate(rows + [none, none], axis=0))
        msg_ref[g, 240:256] = jnp.concatenate([high, rest], axis=0).astype(BF)
    first = place_ref[4] == 0
    at = pl.ds(pl.multiple_of(place_ref[3] % 2 * 128, 128), 128)
    part = dotf(att_ref[:, at], low, ((1,), (0,)))
    for g in range(8):
        even = part[g * 80 : g * 80 + 40]
        odd = part[g * 80 + 40 : g * 80 + 80]
        mine_ref[g] = jnp.where(first, even, odd).astype(BF)
        theirs_ref[g] = jnp.where(first, odd, even).astype(BF)


def norm_back(place, kept, came, unit, inv, gain, part, att, proj):
    vmem = pl.BlockSpec(memory_space=pltpu.VMEM)
    return pl.pallas_call(
        norm_back_kernel,
        in_specs=[pl.BlockSpec(memory_space=pltpu.SMEM)] + [vmem] * 8,
        out_specs=(vmem,) * 3,
        out_shape=(
            jax.ShapeDtypeStruct((8, 256, 128), BF),
            jax.ShapeDtypeStruct((8, 40, 1280), BF),
            jax.ShapeDtypeStruct((8, 40, 1280), BF),
        ),
        name="norm_back",
    )(place, kept, came, unit, inv, gain, part, att, proj)


def q_tile(own_ref, a):
    pieces = []
    for half in range(2):
        for g in range(8):
            at = a * 32 + half * 16
            pieces.append(own_ref[g, at : at + 16, 160:240])
    return jnp.concatenate(pieces, axis=0)


def fill(own_ref, oth_ref, k_s, v_s, q_s):
    for g in range(8):
        at = g * 256
        k_s[at : at + 128] = own_ref[g, :, 0:80]
        k_s[at + 128 : at + 256] = oth_ref[g, :, 0:80]
        v_s[at : at + 128] = own_ref[g, :, 80:160]
        v_s[at + 128 : at + 256] = oth_ref[g, :, 80:160]
    for a in range(4):
        q_s[a] = q_tile(own_ref, a)


def allowed(core, g, lo, hi):
    row = lax.broadcasted_iota(jnp.int32, (256, 1), 0)
    row = jnp.where(row < 128, row + core * 128, row - core * 128) + g * 256
    return (row >= lo) & (row < hi)


def forward_kernel(core_ref, own_ref, oth_ref, lo_ref, hi_ref, low_ref, full_ref, top_ref, inv_ref, k_s, v_s, q_s, s_s):
    a = pl.program_id(0)

    @pl.when(a == 0)
    def _():
        fill(own_ref, oth_ref, k_s, v_s, q_s)

    core = core_ref[0]
    q = q_s[a]
    lo, hi = lo_ref[0], hi_ref[0]
    top = jnp.full((1, 256), -1e30, F32)
    for g in range(8):
        at = slice(g * 256, (g + 1) * 256)
        s = dotf(k_s[at], q, ((1,), (1,)))
        s = jnp.where(allowed(core, g, lo, hi), s, -1e30)
        s_s[at] = s
        top = jnp.maximum(top, jnp.max(s, axis=0, keepdims=True))
    total = jnp.zeros((1, 256), F32)
    acc = jnp.zeros((HEAD_DIM, 256), F32)
    for g in range(8):
        at = slice(g * 256, (g + 1) * 256)
        p = jnp.exp2((s_s[at] - top) * (SCALE * LOG2E))
        total = total + jnp.sum(p, axis=0, keepdims=True)
        acc = acc + dotf(v_s[at], p.astype(BF), ((0,), (0,)))
    inv = 1.0 / total
    out = acc * inv
    low = out.astype(BF)
    low_ref[0] = low
    low_ref[1] = low
    full_ref[0] = out
    top_ref[0] = top
    inv_ref[0] = inv


def head_forward(core, own, oth, lo, hi):
    whole = pl.BlockSpec((8, 128, 256), lambda a: (0, 0, 0))
    line = pl.BlockSpec((1, 1, 256), lambda a: (a, 0, 0))
    return pl.pallas_call(
        forward_kernel,
        grid=(4,),
        in_specs=[pl.BlockSpec(memory_space=pltpu.SMEM), whole, whole, line, line],
        out_specs=(
            pl.BlockSpec((2, HEAD_DIM, 256), lambda a: (a, 0, 0)),
            pl.BlockSpec((1, HEAD_DIM, 256), lambda a: (a, 0, 0)),
            line,
            line,
        ),
        out_shape=(
            jax.ShapeDtypeStruct((8, HEAD_DIM, 256), BF),
            jax.ShapeDtypeStruct((4, HEAD_DIM, 256), F32),
            jax.ShapeDtypeStruct((4, 1, 256), F32),
            jax.ShapeDtypeStruct((4, 1, 256), F32),
        ),
        scratch_shapes=[
            pltpu.VMEM((2048, HEAD_DIM), BF),
            pltpu.VMEM((2048, HEAD_DIM), BF),
            pltpu.VMEM((4, 256, HEAD_DIM), BF),
            pltpu.VMEM((2048, 256), F32),
        ],
        name="head_forward",
    )(core, own, oth, lo, hi)


def backward_kernel(
    core_ref, own_ref, oth_ref, lo_ref, hi_ref, grad_ref, full_ref, top_ref, inv_ref, keep_ref, send_ref, k_s, v_s, q_s, dk_s, dv_s, dq_s
):
    a = pl.program_id(0)

    @pl.when(a == 0)
    def _():
        fill(own_ref, oth_ref, k_s, v_s, q_s)
        dk_s[...] = jnp.zeros_like(dk_s)
        dv_s[...] = jnp.zeros_like(dv_s)

    core = core_ref[0]
    q = q_s[a]
    lo, hi, top, inv = lo_ref[0], hi_ref[0], top_ref[0], inv_ref[0]
    grad = jnp.concatenate([grad_ref[0], grad_ref[1]], axis=1)
    delta = jnp.sum(grad.astype(F32) * full_ref[0], axis=0, keepdims=True)
    dq = jnp.zeros((HEAD_DIM, 256), F32)
    for g in range(8):
        at = slice(g * 256, (g + 1) * 256)
        s = dotf(k_s[at], q, ((1,), (1,)))
        p = jnp.exp2((s - top) * (SCALE * LOG2E)) * inv
        p = jnp.where(allowed(core, g, lo, hi), p, 0.0)
        dp = dotf(v_s[at], grad, ((1,), (0,)))
        ds = (p * ((dp - delta) * SCALE)).astype(BF)
        dv_s[at] += dotf(p.astype(BF), grad, ((1,), (1,)))
        dk_s[at] += dotf(ds, q, ((1,), (0,)))
        dq = dq + dotf(k_s[at], ds, ((0,), (0,)))
    dq_s[a] = dq.T

    @pl.when(a == 3)
    def _():
        pad = jnp.zeros((128, 16), F32)
        for g in range(8):
            at = g * 256
            parts = []
            for b in range(4):
                for half in range(2):
                    row = half * 128 + g * 16
                    parts.append(dq_s[b, row : row + 16])
            mine = jnp.concatenate(parts, axis=0)
            keep_ref[g] = jnp.concatenate([dk_s[at : at + 128], dv_s[at : at + 128], mine, pad], axis=1).astype(BF)
            send_ref[g] = jnp.concatenate(
                [dk_s[at + 128 : at + 256], dv_s[at + 128 : at + 256], jnp.zeros((128, 96), F32)], axis=1
            ).astype(BF)


def head_backward(core, own, oth, lo, hi, grad, full, top, inv):
    whole = pl.BlockSpec((8, 128, 256), lambda a: (0, 0, 0))
    line = pl.BlockSpec((1, 1, 256), lambda a: (a, 0, 0))
    out = jax.ShapeDtypeStruct((8, 128, 256), BF)
    return pl.pallas_call(
        backward_kernel,
        grid=(4,),
        in_specs=[
            pl.BlockSpec(memory_space=pltpu.SMEM),
            whole,
            whole,
            line,
            line,
            pl.BlockSpec((2, HEAD_DIM, 128), lambda a: (a, 0, 0)),
            pl.BlockSpec((1, HEAD_DIM, 256), lambda a: (a, 0, 0)),
            line,
            line,
        ],
        out_specs=(whole, whole),
        out_shape=(out, out),
        scratch_shapes=[
            pltpu.VMEM((2048, HEAD_DIM), BF),
            pltpu.VMEM((2048, HEAD_DIM), BF),
            pltpu.VMEM((4, 256, HEAD_DIM), BF),
            pltpu.VMEM((2048, HEAD_DIM), F32),
            pltpu.VMEM((2048, HEAD_DIM), F32),
            pltpu.VMEM((4, 256, HEAD_DIM), F32),
        ],
        name="head_backward",
    )(core, own, oth, lo, hi, grad, full, top, inv)


def image_kernel(in_ref, cot_ref, gain_ref, row_ref, out_ref):
    total = jnp.zeros((32, 1), F32)
    for b in range(4):
        block = (in_ref[b].astype(F32) + in_ref[4 + b].astype(F32)) + (in_ref[8 + b].astype(F32) + in_ref[12 + b].astype(F32))
        block = block.astype(BF)
        for n in range(4):
            at = (4 * n + b) * 256
            row_ref[:, at : at + 256] = block[:, n * 256 : (n + 1) * 256]
        block = block.astype(F32)
        total = total + jnp.sum(block * block, axis=1, keepdims=True)
    inv = lax.rsqrt(total * (1.0 / 4096) + EPS)
    scaled = row_ref[...].astype(F32) * inv
    raised = cot_ref[...] * gain_ref[...]
    mean = jnp.sum(raised * scaled, axis=1, keepdims=True) * (1.0 / 4096)
    grad = (inv * (raised - scaled * mean)).astype(BF)
    for b in range(4):
        for n in range(4):
            at = (4 * n + b) * 256
            piece = grad[:, at : at + 256]
            for a in range(4):
                out_ref[4 * a + b, :, n * 256 : (n + 1) * 256] = piece


def image_rows(arrived, cotangent, gain):
    return pl.pallas_call(
        image_kernel,
        out_shape=(jax.ShapeDtypeStruct((32, 4096), BF), jax.ShapeDtypeStruct((16, 32, 1024), BF)),
        name="image_rows",
    )(arrived, cotangent, gain)


def by_half(x):
    inside = x.shape[2:]
    return jnp.moveaxis(x.reshape(8, 2, 16, *inside), 1, 0).reshape(256, *inside)


def slots_of(block):
    pair = block[:, :32, 240:242].astype(F32)
    return by_half(pair[:, :, 0] * 128.0 + pair[:, :, 1]).astype(jnp.int32)


def program(
    patch_rows,
    query,
    key_rows,
    value_rows,
    image_lengths,
    token_slots,
    out_proj,
    merge_gain,
    merger_weight,
    text_rows,
    norm_gain,
    out_grad,
):
    core = lax.axis_index(CORE)
    low_x = lax.axis_index("fsdp_1") % 2
    place = lax.axis_index(FSDP)

    slots = jnp.pad(token_slots[0], (0, 96))[:, None]
    pack, rows_out = packed(query[0], key_rows[0], value_rows[0], patch_rows[0], slots, out_proj)
    own = exchanged(pack, CHIPS)
    oth = other_core(own)
    where = jnp.stack([lax.axis_index(n) for n in EVERY]).astype(jnp.int32)
    weight = gathered_weight(merger_weight, where)
    rows_own = exchanged(rows_out, CHIPS)
    rows_oth = other_core(rows_own)

    lengths = image_lengths[0] * 4
    ends = jnp.cumsum(lengths)
    column = jnp.arange(256, dtype=jnp.int32)
    half, owner, inside = column // 128, column // 16 % 8, column % 16
    index = (2 * owner + core) * 128 + 4 * (half * 16 + inside)
    index = index[None, :] + jnp.arange(4, dtype=jnp.int32)[:, None]
    past = index[:, :, None] >= ends
    lo = jnp.sum(jnp.where(past, lengths, 0), axis=-1)
    hi = jnp.min(jnp.where(past, 2048, ends), axis=-1)
    lo, hi = lo[:, None, :], hi[:, None, :]
    core_scalar = core.astype(jnp.int32)[None]
    att_out, att_full, top, inv = head_forward(core_scalar, own, oth, lo, hi)
    att_own = exchanged(att_out, CHIPS).reshape(640, 256)
    att_oth = other_core(att_own)

    slots_all = jnp.concatenate([slots_of(own), slots_of(oth)], axis=0)
    rank = jnp.sum((slots_all[None, :] < slots_all[:, None]).astype(jnp.int32), axis=1)
    order = (rank[None, :] == jnp.arange(512, dtype=jnp.int32)[:, None]).astype(BF)
    normed, partial, unit, inv_std, proj = project(
        where, att_own, att_oth, rows_own, rows_oth, merge_gain[None], order, weight
    )
    arrived = exchanged(partial, FSDP)

    text = text_rows[0]
    cotangent = out_grad[0]
    token = place * 128 + jnp.arange(128, dtype=jnp.int32)
    is_image = jnp.any(slots_all[None, :] == token[:, None], axis=1)
    before = jnp.sum(
        ((slots_all[None, :] >= place * 128) & (slots_all[None, :] < token[:, None])).astype(jnp.int32), axis=1
    )
    spread = (is_image[:, None] & (before[:, None] == jnp.arange(32, dtype=jnp.int32))).astype(BF)
    image_cot = dotf(spread, cotangent, ((0,), (0,)))
    projected, image_grad = image_rows(arrived, image_cot, norm_gain[None])
    grads = exchanged(image_grad, FSDP).reshape(512, 1024)

    stream = jnp.where(is_image[:, None], dotf(spread, projected, ((1,), (0,))), text.astype(F32))
    inv_rms = lax.rsqrt(jnp.mean(stream * stream, axis=-1, keepdims=True) + EPS)
    scaled = stream * inv_rms
    llm_input = (scaled * norm_gain).astype(BF)
    norm_gain_part = jnp.sum(cotangent.astype(F32) * scaled, axis=0)

    back_own, back_oth = project_back(grads, order, weight)
    crossed = other_core(back_oth)
    first = back_own.astype(F32) + crossed.astype(F32)
    kept = lax.dynamic_slice_in_dim(first, low_x * 128, 128)
    sent = lax.dynamic_slice_in_dim(first, (1 - low_x) * 128, 128)
    came = other_x(sent.astype(BF))
    chunks = merger_blocks(normed, grads)
    merger_grad = section_sum(chunks, where[1], where[0])

    message, mine, theirs = norm_back(
        where, kept, came, unit, inv_std, merge_gain[None], norm_gain_part[None], att_own, proj
    )
    grad_in = exchanged(message, CHIPS)

    keep, send = head_backward(core_scalar, own, oth, lo, hi, grad_in, att_full, top, inv)
    gains = jnp.sum(grad_in[:, 240:256].astype(F32).reshape(8, 2, 8, 128), axis=(0, 1))
    gains = jnp.sum(to_all(gains, SECTION + (CORE,)), axis=0)
    summed = merged_grads(keep, other_core(send), gains)
    returned = exchanged(summed, CHIPS)
    patch_grad, query_grad, key_grad, value_grad, norm_total, merge_total = unpacked(returned, grad_in)

    part = (mine.astype(F32) + other_core(theirs).astype(F32)).astype(BF).reshape(2, 4, 40, 1280)
    mine = lax.dynamic_index_in_dim(part, where[2], keepdims=False)
    theirs = lax.dynamic_index_in_dim(part, 1 - where[2], keepdims=False)
    part = (mine.astype(F32) + flipped(theirs, "fsdp_0", 1).astype(F32)).astype(BF)
    total = lax.dynamic_index_in_dim(part, where[3], keepdims=False).astype(F32)
    for far in (1, 2, 3):
        theirs = lax.dynamic_index_in_dim(part, (where[3] + far) % 4, keepdims=False)
        came_x = shifted(theirs, "fsdp_1", far)
        total = total + came_x.astype(F32)
    proj_grad = all_sum(total.astype(BF), IN_SECTION).astype(F32)

    return (
        llm_input[None],
        patch_grad[None],
        query_grad[None],
        key_grad[None],
        value_grad[None],
        norm_total.reshape(4096),
        merge_total.reshape(2048)[:1280],
        merger_grad,
        proj_grad,
    )


def solution(mesh):
    torus = Mesh(
        mesh.devices.reshape(2, 8, 2, 4, 2),
        ("section_0", "section_1", "fsdp_0", "fsdp_1", "fsdp_2"),
    )
    rows = P(SECTION, FSDP, None)
    placed = (
        rows,
        rows,
        rows,
        rows,
        P(SECTION, None),
        P(SECTION, FSDP),
        P(FSDP, None),
        P(),
        P(SECTION, FSDP),
        rows,
        P(),
        rows,
    )
    return jax.shard_map(
        program,
        mesh=torus,
        in_specs=placed,
        out_specs=(rows, rows, rows, rows, rows, P(), P(), P(SECTION, FSDP), P(FSDP, None)),
        check_vma=False,
    )
```

```python
import jax
import jax.numpy as jnp
from jax import lax
from jax.experimental import pallas as pl
from jax.experimental.pallas import tpu as pltpu
from jax.sharding import Mesh
from jax.sharding import PartitionSpec as P


HEAD_DIM = 80
FSDP = ("fsdp_0", "fsdp_1", "fsdp_2")
CHIPS = ("fsdp_0", "fsdp_1")
CORE = "fsdp_2"
SECTION = ("section_0", "section_1")
EVERY = SECTION + FSDP
EPS = 1e-06
LOG2E = 1.4426950408889634
SCALE = HEAD_DIM**-0.5
BF = jnp.bfloat16
F32 = jnp.float32


def dotf(a, b, dims):
    return lax.dot_general(a, b, (dims, ((), ())), preferred_element_type=F32)


def exchanged(x, axis):
    return lax.all_to_all(x, axis, split_axis=0, concat_axis=0, tiled=True)


def to_all(x, axis):
    return exchanged(jnp.broadcast_to(x, (lax.axis_size(axis), *x.shape)), axis)


def other_core(x):
    return lax.ppermute(x, CORE, [(0, 1), (1, 0)])


def other_x(x):
    return lax.ppermute(x, "fsdp_1", [(0, 1), (1, 0), (2, 3), (3, 2)])


def shifted(x, axis, by):
    n = lax.axis_size(axis)
    return lax.ppermute(x, axis, [(i, (i + by) % n) for i in range(n)])


def flipped(x, axis, bit):
    return lax.ppermute(x, axis, [(i, i ^ bit) for i in range(lax.axis_size(axis))])


def swapped(x, flip=0):
    pairs = []
    for i in range(256):
        core, low_x, high_x, y = i % 2, i // 2 % 2, i // 4 % 2, i // 8 % 2
        r, q, top = i // 16 % 4, i // 64 % 2, i // 128
        target = ((((y * 2 + high_x) * 4 + r) * 2 + top) * 2 + q) * 4 + low_x * 2 + core
        pairs.append((i, target ^ (flip * 128)))
    return lax.ppermute(x, EVERY, pairs)


def swapped_back(x, flip=0):
    pairs = []
    for i in range(256):
        j = i ^ (flip * 128)
        core, low_x, high_x, y = j % 2, j // 2 % 2, j // 4 % 2, j // 8 % 2
        r, q, top = j // 16 % 4, j // 64 % 2, j // 128
        target = ((((y * 2 + high_x) * 4 + r) * 2 + top) * 2 + q) * 4 + low_x * 2 + core
        pairs.append((i, target))
    return lax.ppermute(x, EVERY, pairs)


def up(x):
    return shifted(x, "section_1", 1)


def down(x):
    return shifted(x, "section_1", -1)


def weight_blocks(block):
    near = swapped(block)
    other = swapped(block, 1)
    at0 = jnp.stack([near, other])
    below1 = up(at0)
    above1 = down(at0)
    below2 = up(below1)
    above2 = down(above1)
    below3 = up(below2)
    above3 = down(above2)
    far0 = up(below3[0])
    far1 = down(above3[1])
    return at0, above1, above2, above3, far0, far1, below3, below2, below1


def weight_kernel(place_ref, *refs):
    blocks, out_ref = refs[:-1], refs[-1]
    top, z = place_ref[0], place_ref[1]

    def put(block, far, other):
        to = (z + far) % 8
        n = (top ^ other) * 2 + to // 4
        rows = pl.ds(pl.multiple_of(to % 4 * 320, 320), 320)
        out_ref[rows, pl.ds(pl.multiple_of(n * 256, 256), 256)] = block

    at0, above1, above2, above3, far0, far1, below3, below2, below1 = blocks
    for far, ref in ((0, at0), (1, above1), (2, above2), (3, above3), (5, below3), (6, below2), (7, below1)):
        put(ref[0], far, 0)
        put(ref[1], far, 1)
    put(far0[...], 4, 0)
    put(far1[...], 4, 1)


def gathered_weight(block, place):
    blocks = weight_blocks(block)
    vmem = pl.BlockSpec(memory_space=pltpu.VMEM)
    return pl.pallas_call(
        weight_kernel,
        in_specs=[pl.BlockSpec(memory_space=pltpu.SMEM)] + [vmem] * 9,
        out_specs=vmem,
        out_shape=jax.ShapeDtypeStruct((1280, 1024), BF),
        cost_estimate=pl.CostEstimate(flops=0, bytes_accessed=5242880, transcendentals=0),
        name="weight",
    )(place, *blocks)


def section_sum(chunks, top):
    total = chunks[0].astype(F32)
    came = []
    for far in (1, 7, 2, 6, 3, 5, 4):
        came.append(shifted(chunks[far], "section_1", far))
    for block in came:
        total = total + block.astype(F32)
    total = total.astype(BF)
    near = lax.dynamic_index_in_dim(total, top, keepdims=False)
    other = lax.dynamic_index_in_dim(total, 1 - top, keepdims=False)
    return swapped_back(near).astype(F32) + swapped_back(other, 1).astype(F32)


def all_sum(x, steps):
    for axis, bit in steps:
        came = flipped(x, axis, bit)
        x = (x.astype(F32) + came.astype(F32)).astype(x.dtype)
    return x


IN_SECTION = (("section_1", 1), ("section_1", 2), ("section_1", 4), ("section_0", 1))


def by_patch(dtype, shape=(128, 128)):
    row = lax.broadcasted_iota(jnp.int32, shape, 0)
    col = lax.broadcasted_iota(jnp.int32, shape, 1)
    return (col == 4 * (row % 32) + row // 32).astype(dtype)


def pack_kernel(q_ref, k_ref, v_ref, x_ref, slot_ref, proj_ref, out_ref, rows_ref):
    order = by_patch(BF)
    q = dotf(order, q_ref[...], ((1,), (0,)))
    k = k_ref[...].astype(F32)
    v = v_ref[...].astype(F32)
    slots = slot_ref[...]
    high = (slots // 128).astype(F32)
    low = (slots % 128).astype(F32)
    column = lax.broadcasted_iota(jnp.int32, (128, 16), 1)
    extra = jnp.where(column == 0, high, jnp.where(column == 1, low, 0.0))
    for h in range(8):
        at = slice(h * HEAD_DIM, (h + 1) * HEAD_DIM)
        out_ref[h] = jnp.concatenate([k[:, at], v[:, at], q[:, at], extra], axis=1).astype(BF)
    x = dotf(order, x_ref[...], ((1,), (0,))).astype(BF)
    for a in range(4):
        for j in range(2):
            rows_ref[2 * a + j, 0:32] = x[a * 32 : (a + 1) * 32]
            rows_ref[2 * a + j, 32:72] = proj_ref[...]


def packed(q, k, v, x, slots, proj):
    return pl.pallas_call(
        pack_kernel,
        out_shape=(
            jax.ShapeDtypeStruct((8, 128, 256), BF),
            jax.ShapeDtypeStruct((8, 72, 1280), BF),
        ),
        name="pack",
    )(q, k, v, x, slots, proj)


def halves(x):
    high = x.astype(BF).astype(F32)
    return high, x - high


def unpack_kernel(in_ref, msg_ref, p_ref, q_ref, k_ref, v_ref):
    k_ref[...] = jnp.concatenate([in_ref[h][:, 0:80].astype(F32) for h in range(8)], axis=1).astype(BF)
    v_ref[...] = jnp.concatenate([in_ref[h][:, 80:160].astype(F32) for h in range(8)], axis=1).astype(BF)
    q = jnp.concatenate([in_ref[h][:, 160:240].astype(F32) for h in range(8)], axis=1).astype(BF)
    order = by_patch(BF)
    q_ref[...] = dotf(order, q, ((0,), (0,))).astype(BF)
    for j in range(10):
        g = jnp.concatenate([msg_ref[h, 80 + 16 * j : 96 + 16 * j] for h in range(8)], axis=0)
        p_ref[:, j * 128 : (j + 1) * 128] = dotf(order, g, ((0,), (0,))).astype(BF)


def unpacked(x, msg):
    one = jax.ShapeDtypeStruct((128, 640), BF)
    return pl.pallas_call(
        unpack_kernel,
        out_shape=(
            jax.ShapeDtypeStruct((128, 1280), BF),
            one,
            one,
            one,
        ),
        name="unpack",
    )(x, msg)


def project_kernel(
    place_ref, own_ref, oth_ref, rows_own_ref, rows_oth_ref, gain_ref, order_ref, weight_ref,
    normed_ref, part_ref, unit_ref, inv_ref, proj_ref, wide_s, normed_s
):
    first = place_ref[4] == 0
    low_x = place_ref[3] % 2
    for g in range(8):
        mine = rows_own_ref[g, 32:72].astype(F32)
        theirs = rows_oth_ref[g, 32:72].astype(F32)
        wide_s[g * 80 : g * 80 + 40] = jnp.where(first, mine, theirs)
        wide_s[g * 80 + 40 : g * 80 + 80] = jnp.where(first, theirs, mine)
    proj_ref[...] = wide_s[...].astype(BF)
    for core, (att, rows) in enumerate(((own_ref, rows_own_ref), (oth_ref, rows_oth_ref))):

        def norm(half, carry):
            at = pl.ds(pl.multiple_of(half * 128, 128), 128)
            slim = pl.ds(pl.multiple_of(half * 16, 16), 16)
            x = jnp.concatenate([rows[g, slim] for g in range(8)], axis=0).astype(F32)
            mixed = x + dotf(att[:, at], proj_ref[...], ((0,), (0,)))
            centre = mixed - jnp.mean(mixed, axis=-1, keepdims=True)
            inv = lax.rsqrt(jnp.mean(centre * centre, axis=-1, keepdims=True) + EPS)
            unit = centre * inv
            to = pl.ds(pl.multiple_of(core * 256 + half * 128, 128), 128)
            normed_s[to] = (unit * gain_ref[...]).astype(BF)
            if core == 0:

                @pl.when(low_x == half)
                def _():
                    unit_ref[...] = unit
                    inv_ref[...] = inv

            return carry

        lax.fori_loop(0, 2, norm, 0)

    for k in range(5):
        at = slice(k * 256, (k + 1) * 256)
        normed_ref[:, at] = dotf(order_ref[...], normed_s[:, at], ((1,), (0,))).astype(BF)
    for n in range(4):
        at = slice(n * 256, (n + 1) * 256)
        part = dotf(normed_ref[...], weight_ref[:, at], ((1,), (0,))).astype(BF)
        for o in range(16):
            part_ref[o, :, at] = part[o * 32 : (o + 1) * 32]


def project(place, own, oth, rows_own, rows_oth, gain, order, weight):
    vmem = pl.BlockSpec(memory_space=pltpu.VMEM)
    return pl.pallas_call(
        project_kernel,
        in_specs=[pl.BlockSpec(memory_space=pltpu.SMEM)] + [vmem] * 7,
        out_specs=(vmem,) * 5,
        out_shape=(
            jax.ShapeDtypeStruct((512, 1280), BF),
            jax.ShapeDtypeStruct((16, 32, 1024), BF),
            jax.ShapeDtypeStruct((128, 1280), F32),
            jax.ShapeDtypeStruct((128, 1), F32),
            jax.ShapeDtypeStruct((640, 1280), BF),
        ),
        scratch_shapes=[pltpu.VMEM((640, 1280), F32), pltpu.VMEM((512, 1280), BF)],
        name="project",
    )(place, own, oth, rows_own, rows_oth, gain, order, weight)


def back_kernel(grads_ref, order_ref, weight_ref, own_ref, oth_ref, g_s):
    for k in range(4):
        at = slice(k * 256, (k + 1) * 256)
        g_s[:, at] = dotf(order_ref[...], grads_ref[:, at], ((0,), (0,))).astype(BF)
    for k in range(5):
        at = slice(k * 256, (k + 1) * 256)
        part = dotf(g_s[...], weight_ref[at], ((1,), (1,))).astype(BF)
        own_ref[:, at] = part[0:256]
        oth_ref[:, at] = part[256:512]


def project_back(grads, order, weight):
    half = jax.ShapeDtypeStruct((256, 1280), BF)
    return pl.pallas_call(
        back_kernel, out_shape=(half, half), scratch_shapes=[pltpu.VMEM((512, 1024), BF)], name="project_back"
    )(grads, order, weight)


def merger_kernel(place_ref, normed_ref, grads_ref, *refs):
    outs, wide_s = refs[:-1], refs[-1]

    def columns(n, carry):
        at = pl.ds(pl.multiple_of(n * 256, 256), 256)
        wide_s[:, at] = dotf(normed_ref[...], grads_ref[:, at], ((0,), (0,)))
        return carry

    lax.fori_loop(0, 4, columns, 0)
    for far, out_ref in enumerate(outs):
        to = (place_ref[1] + far) % 8
        rows = pl.ds(pl.multiple_of(to % 4 * 320, 320), 320)
        for top in range(2):
            n = top * 2 + to // 4
            out_ref[top] = wide_s[rows, pl.ds(pl.multiple_of(n * 256, 256), 256)].astype(BF)


def merger_blocks(place, normed, grads):
    vmem = pl.BlockSpec(memory_space=pltpu.VMEM)
    return pl.pallas_call(
        merger_kernel,
        in_specs=[pl.BlockSpec(memory_space=pltpu.SMEM), vmem, vmem],
        out_specs=(vmem,) * 8,
        out_shape=(jax.ShapeDtypeStruct((2, 320, 256), BF),) * 8,
        scratch_shapes=[pltpu.VMEM((1280, 1024), F32)],
        name="merger",
    )(place, normed, grads)


def norm_back_kernel(place_ref, kept_ref, came_ref, unit_ref, inv_ref, gain_ref, part_ref, att_ref, proj_ref, msg_ref, mine_ref, theirs_ref):
    grad = kept_ref[...] + came_ref[...].astype(F32)
    unit = unit_ref[...]
    merge_part = jnp.sum(grad * unit, axis=0, keepdims=True)
    raised = grad * gain_ref[...]
    mean = jnp.mean(raised, axis=-1, keepdims=True)
    mixed = inv_ref[...] * (raised - mean - unit * jnp.mean(raised * unit, axis=-1, keepdims=True))
    low = mixed.astype(BF)
    att_grad = dotf(proj_ref[...], low, ((1,), (1,))).astype(BF)
    norm_part = part_ref[...]
    none = jnp.zeros((1, 128), F32)
    for g in range(8):
        msg_ref[g, 0:80] = att_grad[g * 80 : (g + 1) * 80]
        for j in range(10):
            msg_ref[g, 80 + 16 * j : 96 + 16 * j] = low[g * 16 : (g + 1) * 16, j * 128 : (j + 1) * 128]
        rows = [norm_part[:, (4 * g + j) * 128 : (4 * g + j + 1) * 128] for j in range(4)]
        rows += [merge_part[:, (2 * g + j) * 128 : (2 * g + j + 1) * 128] if g < 5 else none for j in range(2)]
        high, rest = halves(jnp.concatenate(rows + [none, none], axis=0))
        msg_ref[g, 240:256] = jnp.concatenate([high, rest], axis=0).astype(BF)
    first = place_ref[4] == 0
    at = pl.ds(pl.multiple_of(place_ref[3] % 2 * 128, 128), 128)
    part = dotf(att_ref[:, at], low, ((1,), (0,)))
    for g in range(8):
        even = part[g * 80 : g * 80 + 40]
        odd = part[g * 80 + 40 : g * 80 + 80]
        mine_ref[g] = jnp.where(first, even, odd).astype(BF)
        theirs_ref[g] = jnp.where(first, odd, even).astype(BF)


def norm_back(place, kept, came, unit, inv, gain, part, att, proj):
    vmem = pl.BlockSpec(memory_space=pltpu.VMEM)
    return pl.pallas_call(
        norm_back_kernel,
        in_specs=[pl.BlockSpec(memory_space=pltpu.SMEM)] + [vmem] * 8,
        out_specs=(vmem,) * 3,
        out_shape=(
            jax.ShapeDtypeStruct((8, 256, 128), BF),
            jax.ShapeDtypeStruct((8, 40, 1280), BF),
            jax.ShapeDtypeStruct((8, 40, 1280), BF),
        ),
        name="norm_back",
    )(place, kept, came, unit, inv, gain, part, att, proj)


def q_tile(own_ref, a):
    pieces = []
    for half in range(2):
        for g in range(8):
            at = a * 32 + half * 16
            pieces.append(own_ref[g, at : at + 16, 160:240])
    return jnp.concatenate(pieces, axis=0)


def fill(own_ref, oth_ref, k_s, v_s, q_s):
    for g in range(8):
        at = g * 256
        k_s[at : at + 128] = own_ref[g, :, 0:80]
        k_s[at + 128 : at + 256] = oth_ref[g, :, 0:80]
        v_s[at : at + 128] = own_ref[g, :, 80:160]
        v_s[at + 128 : at + 256] = oth_ref[g, :, 80:160]
    for a in range(4):
        q_s[a] = q_tile(own_ref, a)


def ranges(length_ref, core, a):
    column = lax.broadcasted_iota(jnp.int32, (1, 256), 1)
    half, owner, inside = column // 128, column // 16 % 8, column % 16
    index = (2 * owner + core) * 128 + 4 * (half * 16 + inside) + a
    start = 0
    lo = jnp.zeros((1, 256), jnp.int32)
    hi = jnp.zeros((1, 256), jnp.int32)
    for k in range(4):
        end = start + 4 * length_ref[0, k]
        lo = jnp.where(index >= start, start, lo)
        hi = jnp.where(index >= start, end, hi)
        start = end
    return lo, hi


def allowed(core, g, lo, hi):
    row = lax.broadcasted_iota(jnp.int32, (256, 1), 0)
    row = jnp.where(row < 128, row + core * 128, row - core * 128) + g * 256
    return (row >= lo) & (row < hi)


def forward_kernel(core_ref, length_ref, own_ref, oth_ref, low_ref, full_ref, top_ref, inv_ref, k_s, v_s, q_s, s_s):
    a = pl.program_id(0)

    @pl.when(a == 0)
    def _():
        fill(own_ref, oth_ref, k_s, v_s, q_s)

    core = core_ref[0]
    q = q_s[a]
    lo, hi = ranges(length_ref, core, a)
    top = jnp.full((1, 256), -1e30, F32)
    for g in range(8):
        at = slice(g * 256, (g + 1) * 256)
        s = dotf(k_s[at], q, ((1,), (1,)))
        s = jnp.where(allowed(core, g, lo, hi), s, -1e30)
        s_s[at] = s
        top = jnp.maximum(top, jnp.max(s, axis=0, keepdims=True))
    total = jnp.zeros((1, 256), F32)
    acc = jnp.zeros((HEAD_DIM, 256), F32)
    for g in range(8):
        at = slice(g * 256, (g + 1) * 256)
        p = jnp.exp2((s_s[at] - top) * (SCALE * LOG2E))
        total = total + jnp.sum(p, axis=0, keepdims=True)
        acc = acc + dotf(v_s[at], p.astype(BF), ((0,), (0,)))
    inv = 1.0 / total
    out = acc * inv
    low = out.astype(BF)
    low_ref[0] = low
    low_ref[1] = low
    full_ref[0] = out
    top_ref[0] = top
    inv_ref[0] = inv


def head_forward(core, lengths, own, oth):
    whole = pl.BlockSpec((8, 128, 256), lambda a: (0, 0, 0))
    line = pl.BlockSpec((1, 1, 256), lambda a: (a, 0, 0))
    return pl.pallas_call(
        forward_kernel,
        grid=(4,),
        in_specs=[pl.BlockSpec(memory_space=pltpu.SMEM)] * 2 + [whole, whole],
        out_specs=(
            pl.BlockSpec((2, HEAD_DIM, 256), lambda a: (a, 0, 0)),
            pl.BlockSpec((1, HEAD_DIM, 256), lambda a: (a, 0, 0)),
            line,
            line,
        ),
        out_shape=(
            jax.ShapeDtypeStruct((8, HEAD_DIM, 256), BF),
            jax.ShapeDtypeStruct((4, HEAD_DIM, 256), F32),
            jax.ShapeDtypeStruct((4, 1, 256), F32),
            jax.ShapeDtypeStruct((4, 1, 256), F32),
        ),
        scratch_shapes=[
            pltpu.VMEM((2048, HEAD_DIM), BF),
            pltpu.VMEM((2048, HEAD_DIM), BF),
            pltpu.VMEM((4, 256, HEAD_DIM), BF),
            pltpu.VMEM((2048, 256), F32),
        ],
        name="head_forward",
    )(core, lengths, own, oth)


def backward_kernel(
    core_ref, length_ref, own_ref, oth_ref, grad_ref, full_ref, top_ref, inv_ref, keep_ref, send_ref, k_s, v_s, q_s, dk_s, dv_s, dq_s
):
    a = pl.program_id(0)

    @pl.when(a == 0)
    def _():
        fill(own_ref, oth_ref, k_s, v_s, q_s)
        dk_s[...] = jnp.zeros_like(dk_s)
        dv_s[...] = jnp.zeros_like(dv_s)

    core = core_ref[0]
    q = q_s[a]
    lo, hi = ranges(length_ref, core, a)
    top, inv = top_ref[0], inv_ref[0]
    grad = jnp.concatenate([grad_ref[0], grad_ref[1]], axis=1)
    delta = jnp.sum(grad.astype(F32) * full_ref[0], axis=0, keepdims=True)
    dq = jnp.zeros((HEAD_DIM, 256), F32)
    for g in range(8):
        at = slice(g * 256, (g + 1) * 256)
        s = dotf(k_s[at], q, ((1,), (1,)))
        p = jnp.exp2((s - top) * (SCALE * LOG2E)) * inv
        p = jnp.where(allowed(core, g, lo, hi), p, 0.0)
        dp = dotf(v_s[at], grad, ((1,), (0,)))
        ds = (p * ((dp - delta) * SCALE)).astype(BF)
        dv_s[at] += dotf(p.astype(BF), grad, ((1,), (1,)))
        dk_s[at] += dotf(ds, q, ((1,), (0,)))
        dq = dq + dotf(k_s[at], ds, ((0,), (0,)))
    dq_s[a] = dq.T

    @pl.when(a == 3)
    def _():
        pad = jnp.zeros((128, 16), F32)
        for g in range(8):
            at = g * 256
            parts = []
            for b in range(4):
                for half in range(2):
                    row = half * 128 + g * 16
                    parts.append(dq_s[b, row : row + 16])
            mine = jnp.concatenate(parts, axis=0)
            keep_ref[g] = jnp.concatenate([dk_s[at : at + 128], dv_s[at : at + 128], mine, pad], axis=1).astype(BF)
            send_ref[g] = jnp.concatenate(
                [dk_s[at + 128 : at + 256], dv_s[at + 128 : at + 256], jnp.zeros((128, 96), F32)], axis=1
            ).astype(BF)


def head_backward(core, lengths, own, oth, grad, full, top, inv):
    whole = pl.BlockSpec((8, 128, 256), lambda a: (0, 0, 0))
    line = pl.BlockSpec((1, 1, 256), lambda a: (a, 0, 0))
    out = jax.ShapeDtypeStruct((8, 128, 256), BF)
    return pl.pallas_call(
        backward_kernel,
        grid=(4,),
        in_specs=[
            pl.BlockSpec(memory_space=pltpu.SMEM),
            pl.BlockSpec(memory_space=pltpu.SMEM),
            whole,
            whole,
            pl.BlockSpec((2, HEAD_DIM, 128), lambda a: (a, 0, 0)),
            pl.BlockSpec((1, HEAD_DIM, 256), lambda a: (a, 0, 0)),
            line,
            line,
        ],
        out_specs=(whole, whole),
        out_shape=(out, out),
        scratch_shapes=[
            pltpu.VMEM((2048, HEAD_DIM), BF),
            pltpu.VMEM((2048, HEAD_DIM), BF),
            pltpu.VMEM((4, 256, HEAD_DIM), BF),
            pltpu.VMEM((2048, HEAD_DIM), F32),
            pltpu.VMEM((2048, HEAD_DIM), F32),
            pltpu.VMEM((4, 256, HEAD_DIM), F32),
        ],
        name="head_backward",
    )(core, lengths, own, oth, grad, full, top, inv)


def image_kernel(in_ref, cot_ref, gain_ref, row_ref, out_ref):
    total = jnp.zeros((32, 1), F32)
    for b in range(4):
        block = (in_ref[b].astype(F32) + in_ref[4 + b].astype(F32)) + (in_ref[8 + b].astype(F32) + in_ref[12 + b].astype(F32))
        block = block.astype(BF)
        for n in range(4):
            at = (4 * n + b) * 256
            row_ref[:, at : at + 256] = block[:, n * 256 : (n + 1) * 256]
        block = block.astype(F32)
        total = total + jnp.sum(block * block, axis=1, keepdims=True)
    inv = lax.rsqrt(total * (1.0 / 4096) + EPS)
    scaled = row_ref[...].astype(F32) * inv
    raised = cot_ref[...] * gain_ref[...]
    mean = jnp.sum(raised * scaled, axis=1, keepdims=True) * (1.0 / 4096)
    grad = (inv * (raised - scaled * mean)).astype(BF)
    for b in range(4):
        for n in range(4):
            at = (4 * n + b) * 256
            piece = grad[:, at : at + 256]
            for a in range(4):
                out_ref[4 * a + b, :, n * 256 : (n + 1) * 256] = piece


def image_rows(arrived, cotangent, gain):
    return pl.pallas_call(
        image_kernel,
        out_shape=(jax.ShapeDtypeStruct((32, 4096), BF), jax.ShapeDtypeStruct((16, 32, 1024), BF)),
        name="image_rows",
    )(arrived, cotangent, gain)


def token_kernel(text_ref, row_ref, spread_ref, cot_ref, gain_ref, out_ref, part_ref):
    spread = spread_ref[...]
    is_image = jnp.sum(spread.astype(F32), axis=1, keepdims=True) > 0.5

    def fill(k, total):
        at = pl.ds(pl.multiple_of(k * 512, 512), 512)
        rows = dotf(spread, row_ref[:, at], ((1,), (0,)))
        stream = jnp.where(is_image, rows, text_ref[:, at].astype(F32))
        out_ref[:, at] = stream.astype(BF)
        return total + jnp.sum(stream * stream, axis=1, keepdims=True)

    total = lax.fori_loop(0, 8, fill, jnp.zeros((128, 1), F32))
    inv = lax.rsqrt(total * (1.0 / 4096) + EPS)

    def scale(k, carry):
        at = pl.ds(pl.multiple_of(k * 512, 512), 512)
        scaled = out_ref[:, at].astype(F32) * inv
        part_ref[:, at] = jnp.sum(cot_ref[:, at].astype(F32) * scaled, axis=0, keepdims=True)
        out_ref[:, at] = (scaled * gain_ref[:, at]).astype(BF)
        return carry

    lax.fori_loop(0, 8, scale, 0)


def token_rows(text, rows, spread, cotangent, gain):
    return pl.pallas_call(
        token_kernel,
        out_shape=(jax.ShapeDtypeStruct((128, 4096), BF), jax.ShapeDtypeStruct((1, 4096), F32)),
        name="token_rows",
    )(text, rows, spread, cotangent, gain)


def by_half(x):
    inside = x.shape[2:]
    return jnp.moveaxis(x.reshape(8, 2, 16, *inside), 1, 0).reshape(256, *inside)


def slots_of(block):
    pair = block[:, :32, 240:242].astype(F32)
    return by_half(pair[:, :, 0] * 128.0 + pair[:, :, 1]).astype(jnp.int32)


def program(
    patch_rows,
    query,
    key_rows,
    value_rows,
    image_lengths,
    token_slots,
    out_proj,
    merge_gain,
    merger_weight,
    text_rows,
    norm_gain,
    out_grad,
):
    core = lax.axis_index(CORE)
    low_x = lax.axis_index("fsdp_1") % 2
    place = lax.axis_index(FSDP)

    slots = jnp.pad(token_slots[0], (0, 96))[:, None]
    pack, rows_out = packed(query[0], key_rows[0], value_rows[0], patch_rows[0], slots, out_proj)
    own = exchanged(pack, CHIPS)
    oth = other_core(own)
    where = jnp.stack([lax.axis_index(n) for n in EVERY]).astype(jnp.int32)
    weight = gathered_weight(merger_weight, where)
    rows_own = exchanged(rows_out, CHIPS)
    rows_oth = other_core(rows_own)

    core_scalar = core.astype(jnp.int32)[None]
    att_out, att_full, top, inv = head_forward(core_scalar, image_lengths, own, oth)
    att_own = exchanged(att_out, CHIPS).reshape(640, 256)
    att_oth = other_core(att_own)

    slots_all = jnp.concatenate([slots_of(own), slots_of(oth)], axis=0)
    rank = jnp.sum((slots_all[None, :] < slots_all[:, None]).astype(jnp.int32), axis=1)
    order = (rank[None, :] == jnp.arange(512, dtype=jnp.int32)[:, None]).astype(BF)
    normed, partial, unit, inv_std, proj = project(
        where, att_own, att_oth, rows_own, rows_oth, merge_gain[None], order, weight
    )
    arrived = exchanged(partial, FSDP)

    text = text_rows[0]
    cotangent = out_grad[0]
    token = place * 128 + jnp.arange(128, dtype=jnp.int32)
    is_image = jnp.any(slots_all[None, :] == token[:, None], axis=1)
    before = jnp.sum(
        ((slots_all[None, :] >= place * 128) & (slots_all[None, :] < token[:, None])).astype(jnp.int32), axis=1
    )
    spread = (is_image[:, None] & (before[:, None] == jnp.arange(32, dtype=jnp.int32))).astype(BF)
    image_cot = dotf(spread, cotangent, ((0,), (0,)))
    projected, image_grad = image_rows(arrived, image_cot, norm_gain[None])
    grads = exchanged(image_grad, FSDP).reshape(512, 1024)

    llm_input, norm_gain_part = token_rows(text, projected, spread, cotangent, norm_gain[None])

    back_own, back_oth = project_back(grads, order, weight)
    crossed = other_core(back_oth)
    first = back_own.astype(F32) + crossed.astype(F32)
    kept = lax.dynamic_slice_in_dim(first, low_x * 128, 128)
    sent = lax.dynamic_slice_in_dim(first, (1 - low_x) * 128, 128)
    came = other_x(sent.astype(BF))
    chunks = merger_blocks(where, normed, grads)
    merger_grad = section_sum(chunks, where[0])

    message, mine, theirs = norm_back(where, kept, came, unit, inv_std, merge_gain[None], norm_gain_part, att_own, proj)
    grad_in = exchanged(message, CHIPS)

    keep, send = head_backward(core_scalar, image_lengths, own, oth, grad_in, att_full, top, inv)
    summed = (keep.astype(F32) + other_core(send).astype(F32)).astype(BF)
    returned = exchanged(summed, CHIPS)
    gains = jnp.sum(grad_in[:, 240:256].astype(F32).reshape(8, 2, 8, 128), axis=(0, 1))
    patch_grad, query_grad, key_grad, value_grad = unpacked(returned, grad_in)
    part = (mine.astype(F32) + other_core(theirs).astype(F32)).astype(BF).reshape(2, 4, 40, 1280)
    mine = lax.dynamic_index_in_dim(part, where[2], keepdims=False)
    theirs = lax.dynamic_index_in_dim(part, 1 - where[2], keepdims=False)
    part = (mine.astype(F32) + flipped(theirs, "fsdp_0", 1).astype(F32)).astype(BF)
    total = lax.dynamic_index_in_dim(part, where[3], keepdims=False).astype(F32)
    for far in (1, 2, 3):
        theirs = lax.dynamic_index_in_dim(part, (where[3] + far) % 4, keepdims=False)
        came_x = shifted(theirs, "fsdp_1", far)
        total = total + came_x.astype(F32)
    total = jnp.concatenate([total, jnp.pad(gains, ((0, 0), (0, 1152)))], axis=0).astype(BF)
    total = all_sum(total, IN_SECTION)
    proj_grad = total[:40].astype(F32)
    gains = to_all(total[40:, :128], FSDP).astype(F32)
    gains = jnp.sum(gains.reshape(8, 2, 8, 128), axis=1)
    norm_total = gains[:, 0:4].reshape(4096)
    merge_total = gains[:5, 4:6].reshape(1280)

    return (
        llm_input[None],
        patch_grad[None],
        query_grad[None],
        key_grad[None],
        value_grad[None],
        norm_total,
        merge_total,
        merger_grad,
        proj_grad,
    )


def solution(mesh):
    torus = Mesh(
        mesh.devices.reshape(2, 8, 2, 4, 2),
        ("section_0", "section_1", "fsdp_0", "fsdp_1", "fsdp_2"),
    )
    rows = P(SECTION, FSDP, None)
    placed = (
        rows,
        rows,
        rows,
        rows,
        P(SECTION, None),
        P(SECTION, FSDP),
        P(FSDP, None),
        P(),
        P(SECTION, FSDP),
        rows,
        P(),
        rows,
    )
    return jax.shard_map(
        program,
        mesh=torus,
        in_specs=placed,
        out_specs=(rows, rows, rows, rows, rows, P(), P(), P(SECTION, FSDP), P(FSDP, None)),
        check_vma=False,
    )
```

```python
import jax
import jax.numpy as jnp
from jax import lax
from jax.experimental import pallas as pl
from jax.experimental.pallas import tpu as pltpu
from jax.sharding import Mesh
from jax.sharding import PartitionSpec as P


HEAD_DIM = 80
FSDP = ("fsdp_0", "fsdp_1", "fsdp_2")
CHIPS = ("fsdp_0", "fsdp_1")
CORE = "fsdp_2"
SECTION = ("section_0", "section_1")
EVERY = SECTION + FSDP
EPS = 1e-06
LOG2E = 1.4426950408889634
SCALE = HEAD_DIM**-0.5
BF = jnp.bfloat16
F32 = jnp.float32


def dotf(a, b, dims):
    return lax.dot_general(a, b, (dims, ((), ())), preferred_element_type=F32)


def exchanged(x, axis):
    return lax.all_to_all(x, axis, split_axis=0, concat_axis=0, tiled=True)


def other_core(x):
    return lax.ppermute(x, CORE, [(0, 1), (1, 0)])


def other_x(x):
    return lax.ppermute(x, "fsdp_1", [(0, 1), (1, 0), (2, 3), (3, 2)])


def shifted(x, axis, by):
    n = lax.axis_size(axis)
    return lax.ppermute(x, axis, [(i, (i + by) % n) for i in range(n)])


def flipped(x, axis, bit):
    return lax.ppermute(x, axis, [(i, i ^ bit) for i in range(lax.axis_size(axis))])


def swapped(x, flip=0):
    pairs = []
    for i in range(256):
        core, low_x, high_x, y = i % 2, i // 2 % 2, i // 4 % 2, i // 8 % 2
        r, q, top = i // 16 % 4, i // 64 % 2, i // 128
        target = ((((y * 2 + high_x) * 4 + r) * 2 + top) * 2 + q) * 4 + low_x * 2 + core
        pairs.append((i, target ^ (flip * 128)))
    return lax.ppermute(x, EVERY, pairs)


def swapped_back(x, flip=0):
    pairs = []
    for i in range(256):
        j = i ^ (flip * 128)
        core, low_x, high_x, y = j % 2, j // 2 % 2, j // 4 % 2, j // 8 % 2
        r, q, top = j // 16 % 4, j // 64 % 2, j // 128
        target = ((((y * 2 + high_x) * 4 + r) * 2 + top) * 2 + q) * 4 + low_x * 2 + core
        pairs.append((i, target))
    return lax.ppermute(x, EVERY, pairs)


def up(x):
    return shifted(x, "section_1", 1)


def down(x):
    return shifted(x, "section_1", -1)


def weight_blocks(block):
    near = swapped(block)
    other = swapped(block, 1)
    at0 = jnp.stack([near, other])
    below1 = up(at0)
    above1 = down(at0)
    below2 = up(below1)
    above2 = down(above1)
    below3 = up(below2)
    above3 = down(above2)
    far0 = up(below3[0])
    far1 = down(above3[1])
    return at0, above1, above2, above3, far0, far1, below3, below2, below1


def weight_kernel(place_ref, *refs):
    blocks, out_ref = refs[:-1], refs[-1]
    top, z = place_ref[0], place_ref[1]

    def put(block, far, other):
        to = (z + far) % 8
        n = (top ^ other) * 2 + to // 4
        rows = pl.ds(pl.multiple_of(to % 4 * 320, 320), 320)
        out_ref[rows, pl.ds(pl.multiple_of(n * 256, 256), 256)] = block

    at0, above1, above2, above3, far0, far1, below3, below2, below1 = blocks
    for far, ref in ((0, at0), (1, above1), (2, above2), (3, above3), (5, below3), (6, below2), (7, below1)):
        put(ref[0], far, 0)
        put(ref[1], far, 1)
    put(far0[...], 4, 0)
    put(far1[...], 4, 1)


def gathered_weight(block, place):
    blocks = weight_blocks(block)
    vmem = pl.BlockSpec(memory_space=pltpu.VMEM)
    return pl.pallas_call(
        weight_kernel,
        in_specs=[pl.BlockSpec(memory_space=pltpu.SMEM)] + [vmem] * 9,
        out_specs=vmem,
        out_shape=jax.ShapeDtypeStruct((1280, 1024), BF),
        cost_estimate=pl.CostEstimate(flops=0, bytes_accessed=5242880, transcendentals=0),
        name="weight",
    )(place, *blocks)


def section_sum(chunks, top):
    total = chunks[0].astype(F32)
    came = []
    for far in (1, 7, 2, 6, 3, 5, 4):
        came.append(shifted(chunks[far], "section_1", far))
    for block in came:
        total = total + block.astype(F32)
    total = total.astype(BF)
    near = lax.dynamic_index_in_dim(total, top, keepdims=False)
    other = lax.dynamic_index_in_dim(total, 1 - top, keepdims=False)
    return swapped_back(near).astype(F32) + swapped_back(other, 1).astype(F32)


def all_sum(x, steps):
    for axis, bit in steps:
        came = flipped(x, axis, bit)
        x = (x.astype(F32) + came.astype(F32)).astype(x.dtype)
    return x


IN_SECTION = (("section_1", 1), ("section_1", 2), ("section_1", 4), ("section_0", 1))


def by_patch(dtype, shape=(128, 128)):
    row = lax.broadcasted_iota(jnp.int32, shape, 0)
    col = lax.broadcasted_iota(jnp.int32, shape, 1)
    return (col == 4 * (row % 32) + row // 32).astype(dtype)


def pack_kernel(q_ref, k_ref, v_ref, x_ref, slot_ref, proj_ref, out_ref, rows_ref):
    order = by_patch(BF)
    q = dotf(order, q_ref[...], ((1,), (0,)))
    k = k_ref[...].astype(F32)
    v = v_ref[...].astype(F32)
    line = slot_ref[...]
    same = lax.broadcasted_iota(jnp.int32, (128, 32), 0) == lax.broadcasted_iota(jnp.int32, (128, 32), 1)
    slots = jnp.sum(jnp.where(same, line, 0), axis=1, keepdims=True)
    high = (slots // 128).astype(F32)
    low = (slots % 128).astype(F32)
    column = lax.broadcasted_iota(jnp.int32, (128, 16), 1)
    extra = jnp.where(column == 0, high, jnp.where(column == 1, low, 0.0))
    for h in range(8):
        at = slice(h * HEAD_DIM, (h + 1) * HEAD_DIM)
        out_ref[h] = jnp.concatenate([k[:, at], v[:, at], q[:, at], extra], axis=1).astype(BF)
    x = dotf(order, x_ref[...], ((1,), (0,))).astype(BF)
    for a in range(4):
        for j in range(2):
            rows_ref[2 * a + j, 0:32] = x[a * 32 : (a + 1) * 32]
            rows_ref[2 * a + j, 32:72] = proj_ref[...]


def packed(q, k, v, x, slots, proj):
    return pl.pallas_call(
        pack_kernel,
        out_shape=(
            jax.ShapeDtypeStruct((8, 128, 256), BF),
            jax.ShapeDtypeStruct((8, 72, 1280), BF),
        ),
        name="pack",
    )(q, k, v, x, slots, proj)


def halves(x):
    high = x.astype(BF).astype(F32)
    return high, x - high


def merge_kernel(keep_ref, add_ref, gain_ref, out_ref):
    high, low = halves(gain_ref[...])
    gains = jnp.concatenate([high, low], axis=0).T
    for g in range(8):
        both = keep_ref[g].astype(F32) + add_ref[g].astype(F32)
        out_ref[g] = jnp.concatenate([both[:, 0:240], gains], axis=1).astype(BF)


def merged_grads(keep, add, gains):
    return pl.pallas_call(merge_kernel, out_shape=jax.ShapeDtypeStruct((8, 128, 256), BF), name="merge")(keep, add, gains)


def gain_kernel(in_ref, out_ref):
    out_ref[...] = jnp.zeros_like(out_ref)
    for g in range(8):
        both = in_ref[g][:, 240:256].astype(F32).T
        rows = both[0:8] + both[8:16]
        for j in range(6):
            out_ref[g : g + 1, j * 128 : (j + 1) * 128] = rows[j : j + 1]


def gain_rows(x):
    return pl.pallas_call(gain_kernel, out_shape=jax.ShapeDtypeStruct((8, 1280), F32), name="gain_rows")(x)


def unpack_kernel(in_ref, msg_ref, p_ref, q_ref, k_ref, v_ref):
    k_ref[...] = jnp.concatenate([in_ref[h][:, 0:80].astype(F32) for h in range(8)], axis=1).astype(BF)
    v_ref[...] = jnp.concatenate([in_ref[h][:, 80:160].astype(F32) for h in range(8)], axis=1).astype(BF)
    q = jnp.concatenate([in_ref[h][:, 160:240].astype(F32) for h in range(8)], axis=1).astype(BF)
    order = by_patch(BF)
    q_ref[...] = dotf(order, q, ((0,), (0,))).astype(BF)
    for j in range(10):
        g = jnp.concatenate([msg_ref[h, 80 + 16 * j : 96 + 16 * j] for h in range(8)], axis=0)
        p_ref[:, j * 128 : (j + 1) * 128] = dotf(order, g, ((0,), (0,))).astype(BF)


def unpacked(x, msg):
    one = jax.ShapeDtypeStruct((128, 640), BF)
    return pl.pallas_call(
        unpack_kernel,
        out_shape=(
            jax.ShapeDtypeStruct((128, 1280), BF),
            one,
            one,
            one,
        ),
        name="unpack",
    )(x, msg)


def project_kernel(
    place_ref, own_ref, oth_ref, rows_own_ref, rows_oth_ref, gain_ref, order_ref, weight_ref,
    normed_ref, part_ref, unit_ref, inv_ref, proj_ref, wide_s, normed_s
):
    first = place_ref[4] == 0
    low_x = place_ref[3] % 2
    for g in range(8):
        mine = rows_own_ref[g, 32:72].astype(F32)
        theirs = rows_oth_ref[g, 32:72].astype(F32)
        wide_s[g * 80 : g * 80 + 40] = jnp.where(first, mine, theirs)
        wide_s[g * 80 + 40 : g * 80 + 80] = jnp.where(first, theirs, mine)
    proj_ref[...] = wide_s[...].astype(BF)
    for core, (att, rows) in enumerate(((own_ref, rows_own_ref), (oth_ref, rows_oth_ref))):

        def norm(half, carry):
            at = pl.ds(pl.multiple_of(half * 128, 128), 128)
            slim = pl.ds(pl.multiple_of(half * 16, 16), 16)
            x = jnp.concatenate([rows[g, slim] for g in range(8)], axis=0).astype(F32)
            mixed = x + dotf(att[:, at], proj_ref[...], ((0,), (0,)))
            centre = mixed - jnp.mean(mixed, axis=-1, keepdims=True)
            inv = lax.rsqrt(jnp.mean(centre * centre, axis=-1, keepdims=True) + EPS)
            unit = centre * inv
            to = pl.ds(pl.multiple_of(core * 256 + half * 128, 128), 128)
            normed_s[to] = (unit * gain_ref[...]).astype(BF)
            if core == 0:

                @pl.when(low_x == half)
                def _():
                    unit_ref[...] = unit
                    inv_ref[...] = inv

            return carry

        lax.fori_loop(0, 2, norm, 0)

    for k in range(5):
        at = slice(k * 256, (k + 1) * 256)
        normed_ref[:, at] = dotf(order_ref[...], normed_s[:, at], ((1,), (0,))).astype(BF)
    for n in range(4):
        at = slice(n * 256, (n + 1) * 256)
        part = dotf(normed_ref[...], weight_ref[:, at], ((1,), (0,))).astype(BF)
        for o in range(16):
            part_ref[o, :, at] = part[o * 32 : (o + 1) * 32]


def project(place, own, oth, rows_own, rows_oth, gain, order, weight):
    vmem = pl.BlockSpec(memory_space=pltpu.VMEM)
    return pl.pallas_call(
        project_kernel,
        in_specs=[pl.BlockSpec(memory_space=pltpu.SMEM)] + [vmem] * 7,
        out_specs=(vmem,) * 5,
        out_shape=(
            jax.ShapeDtypeStruct((512, 1280), BF),
            jax.ShapeDtypeStruct((16, 32, 1024), BF),
            jax.ShapeDtypeStruct((128, 1280), F32),
            jax.ShapeDtypeStruct((128, 1), F32),
            jax.ShapeDtypeStruct((640, 1280), BF),
        ),
        scratch_shapes=[pltpu.VMEM((640, 1280), F32), pltpu.VMEM((512, 1280), BF)],
        name="project",
    )(place, own, oth, rows_own, rows_oth, gain, order, weight)


def back_kernel(grads_ref, order_ref, weight_ref, own_ref, oth_ref, g_s):
    for k in range(4):
        at = slice(k * 256, (k + 1) * 256)
        g_s[:, at] = dotf(order_ref[...], grads_ref[:, at], ((0,), (0,))).astype(BF)
    for k in range(5):
        at = slice(k * 256, (k + 1) * 256)
        part = dotf(g_s[...], weight_ref[at], ((1,), (1,))).astype(BF)
        own_ref[:, at] = part[0:256]
        oth_ref[:, at] = part[256:512]


def project_back(grads, order, weight):
    half = jax.ShapeDtypeStruct((256, 1280), BF)
    return pl.pallas_call(
        back_kernel, out_shape=(half, half), scratch_shapes=[pltpu.VMEM((512, 1024), BF)], name="project_back"
    )(grads, order, weight)


def merger_kernel(place_ref, normed_ref, grads_ref, *refs):
    outs, wide_s = refs[:-1], refs[-1]

    def columns(n, carry):
        at = pl.ds(pl.multiple_of(n * 256, 256), 256)
        wide_s[:, at] = dotf(normed_ref[...], grads_ref[:, at], ((0,), (0,)))
        return carry

    lax.fori_loop(0, 4, columns, 0)
    for far, out_ref in enumerate(outs):
        to = (place_ref[1] + far) % 8
        rows = pl.ds(pl.multiple_of(to % 4 * 320, 320), 320)
        for top in range(2):
            n = top * 2 + to // 4
            out_ref[top] = wide_s[rows, pl.ds(pl.multiple_of(n * 256, 256), 256)].astype(BF)


def merger_blocks(place, normed, grads):
    vmem = pl.BlockSpec(memory_space=pltpu.VMEM)
    return pl.pallas_call(
        merger_kernel,
        in_specs=[pl.BlockSpec(memory_space=pltpu.SMEM), vmem, vmem],
        out_specs=(vmem,) * 8,
        out_shape=(jax.ShapeDtypeStruct((2, 320, 256), BF),) * 8,
        scratch_shapes=[pltpu.VMEM((1280, 1024), F32)],
        name="merger",
    )(place, normed, grads)


def norm_back_kernel(place_ref, kept_ref, came_ref, unit_ref, inv_ref, gain_ref, part_ref, att_ref, proj_ref, msg_ref, mine_ref, theirs_ref):
    grad = kept_ref[...] + came_ref[...].astype(F32)
    unit = unit_ref[...]
    merge_part = jnp.sum(grad * unit, axis=0, keepdims=True)
    raised = grad * gain_ref[...]
    mean = jnp.mean(raised, axis=-1, keepdims=True)
    mixed = inv_ref[...] * (raised - mean - unit * jnp.mean(raised * unit, axis=-1, keepdims=True))
    low = mixed.astype(BF)
    att_grad = dotf(proj_ref[...], low, ((1,), (1,))).astype(BF)
    norm_part = part_ref[...]
    none = jnp.zeros((1, 128), F32)
    for g in range(8):
        msg_ref[g, 0:80] = att_grad[g * 80 : (g + 1) * 80]
        for j in range(10):
            msg_ref[g, 80 + 16 * j : 96 + 16 * j] = low[g * 16 : (g + 1) * 16, j * 128 : (j + 1) * 128]
        rows = [norm_part[:, (4 * g + j) * 128 : (4 * g + j + 1) * 128] for j in range(4)]
        rows += [merge_part[:, (2 * g + j) * 128 : (2 * g + j + 1) * 128] if g < 5 else none for j in range(2)]
        high, rest = halves(jnp.concatenate(rows + [none, none], axis=0))
        msg_ref[g, 240:256] = jnp.concatenate([high, rest], axis=0).astype(BF)
    first = place_ref[4] == 0
    at = pl.ds(pl.multiple_of(place_ref[3] % 2 * 128, 128), 128)
    part = dotf(att_ref[:, at], low, ((1,), (0,)))
    for g in range(8):
        even = part[g * 80 : g * 80 + 40]
        odd = part[g * 80 + 40 : g * 80 + 80]
        mine_ref[g] = jnp.where(first, even, odd).astype(BF)
        theirs_ref[g] = jnp.where(first, odd, even).astype(BF)


def norm_back(place, kept, came, unit, inv, gain, part, att, proj):
    vmem = pl.BlockSpec(memory_space=pltpu.VMEM)
    return pl.pallas_call(
        norm_back_kernel,
        in_specs=[pl.BlockSpec(memory_space=pltpu.SMEM)] + [vmem] * 8,
        out_specs=(vmem,) * 3,
        out_shape=(
            jax.ShapeDtypeStruct((8, 256, 128), BF),
            jax.ShapeDtypeStruct((8, 40, 1280), BF),
            jax.ShapeDtypeStruct((8, 40, 1280), BF),
        ),
        name="norm_back",
    )(place, kept, came, unit, inv, gain, part, att, proj)


def q_tile(own_ref, a):
    pieces = []
    for half in range(2):
        for g in range(8):
            at = a * 32 + half * 16
            pieces.append(own_ref[g, at : at + 16, 160:240])
    return jnp.concatenate(pieces, axis=0)


def fill(own_ref, oth_ref, k_s, v_s, q_s):
    for g in range(8):
        at = g * 256
        k_s[at : at + 128] = own_ref[g, :, 0:80]
        k_s[at + 128 : at + 256] = oth_ref[g, :, 0:80]
        v_s[at : at + 128] = own_ref[g, :, 80:160]
        v_s[at + 128 : at + 256] = oth_ref[g, :, 80:160]
    for a in range(4):
        q_s[a] = q_tile(own_ref, a)


def ranges(length_ref, core, a):
    column = lax.broadcasted_iota(jnp.int32, (1, 256), 1)
    half, owner, inside = column // 128, column // 16 % 8, column % 16
    index = (2 * owner + core) * 128 + 4 * (half * 16 + inside) + a
    start = 0
    lo = jnp.zeros((1, 256), jnp.int32)
    hi = jnp.zeros((1, 256), jnp.int32)
    for k in range(4):
        end = start + 4 * length_ref[0, k]
        lo = jnp.where(index >= start, start, lo)
        hi = jnp.where(index >= start, end, hi)
        start = end
    return lo, hi


def allowed(core, g, lo, hi):
    row = lax.broadcasted_iota(jnp.int32, (256, 1), 0)
    row = jnp.where(row < 128, row + core * 128, row - core * 128) + g * 256
    return (row >= lo) & (row < hi)


def forward_kernel(core_ref, length_ref, own_ref, oth_ref, low_ref, full_ref, top_ref, inv_ref, k_s, v_s, q_s, s_s):
    a = pl.program_id(0)

    @pl.when(a == 0)
    def _():
        fill(own_ref, oth_ref, k_s, v_s, q_s)

    core = core_ref[0]
    q = q_s[a]
    lo, hi = ranges(length_ref, core, a)
    top = jnp.full((1, 256), -1e30, F32)
    for g in range(8):
        at = slice(g * 256, (g + 1) * 256)
        s = dotf(k_s[at], q, ((1,), (1,)))
        s = jnp.where(allowed(core, g, lo, hi), s, -1e30)
        s_s[at] = s
        top = jnp.maximum(top, jnp.max(s, axis=0, keepdims=True))
    total = jnp.zeros((1, 256), F32)
    acc = jnp.zeros((HEAD_DIM, 256), F32)
    for g in range(8):
        at = slice(g * 256, (g + 1) * 256)
        p = jnp.exp2((s_s[at] - top) * (SCALE * LOG2E))
        total = total + jnp.sum(p, axis=0, keepdims=True)
        acc = acc + dotf(v_s[at], p.astype(BF), ((0,), (0,)))
    inv = 1.0 / total
    out = acc * inv
    low = out.astype(BF)
    low_ref[0] = low
    low_ref[1] = low
    full_ref[0] = out
    top_ref[0] = top
    inv_ref[0] = inv


def head_forward(core, lengths, own, oth):
    whole = pl.BlockSpec((8, 128, 256), lambda a: (0, 0, 0))
    line = pl.BlockSpec((1, 1, 256), lambda a: (a, 0, 0))
    return pl.pallas_call(
        forward_kernel,
        grid=(4,),
        in_specs=[pl.BlockSpec(memory_space=pltpu.SMEM)] * 2 + [whole, whole],
        out_specs=(
            pl.BlockSpec((2, HEAD_DIM, 256), lambda a: (a, 0, 0)),
            pl.BlockSpec((1, HEAD_DIM, 256), lambda a: (a, 0, 0)),
            line,
            line,
        ),
        out_shape=(
            jax.ShapeDtypeStruct((8, HEAD_DIM, 256), BF),
            jax.ShapeDtypeStruct((4, HEAD_DIM, 256), F32),
            jax.ShapeDtypeStruct((4, 1, 256), F32),
            jax.ShapeDtypeStruct((4, 1, 256), F32),
        ),
        scratch_shapes=[
            pltpu.VMEM((2048, HEAD_DIM), BF),
            pltpu.VMEM((2048, HEAD_DIM), BF),
            pltpu.VMEM((4, 256, HEAD_DIM), BF),
            pltpu.VMEM((2048, 256), F32),
        ],
        name="head_forward",
    )(core, lengths, own, oth)


def backward_kernel(
    core_ref, length_ref, own_ref, oth_ref, grad_ref, full_ref, top_ref, inv_ref, keep_ref, send_ref, k_s, v_s, q_s, dk_s, dv_s, dq_s
):
    a = pl.program_id(0)

    @pl.when(a == 0)
    def _():
        fill(own_ref, oth_ref, k_s, v_s, q_s)
        dk_s[...] = jnp.zeros_like(dk_s)
        dv_s[...] = jnp.zeros_like(dv_s)

    core = core_ref[0]
    q = q_s[a]
    lo, hi = ranges(length_ref, core, a)
    top, inv = top_ref[0], inv_ref[0]
    grad = jnp.concatenate([grad_ref[0], grad_ref[1]], axis=1)
    delta = jnp.sum(grad.astype(F32) * full_ref[0], axis=0, keepdims=True)
    dq = jnp.zeros((HEAD_DIM, 256), F32)
    for g in range(8):
        at = slice(g * 256, (g + 1) * 256)
        s = dotf(k_s[at], q, ((1,), (1,)))
        p = jnp.exp2((s - top) * (SCALE * LOG2E)) * inv
        p = jnp.where(allowed(core, g, lo, hi), p, 0.0)
        dp = dotf(v_s[at], grad, ((1,), (0,)))
        ds = (p * ((dp - delta) * SCALE)).astype(BF)
        dv_s[at] += dotf(p.astype(BF), grad, ((1,), (1,)))
        dk_s[at] += dotf(ds, q, ((1,), (0,)))
        dq = dq + dotf(k_s[at], ds, ((0,), (0,)))
    dq_s[a] = dq.T

    @pl.when(a == 3)
    def _():
        pad = jnp.zeros((128, 16), F32)
        for g in range(8):
            at = g * 256
            parts = []
            for b in range(4):
                for half in range(2):
                    row = half * 128 + g * 16
                    parts.append(dq_s[b, row : row + 16])
            mine = jnp.concatenate(parts, axis=0)
            keep_ref[g] = jnp.concatenate([dk_s[at : at + 128], dv_s[at : at + 128], mine, pad], axis=1).astype(BF)
            send_ref[g] = jnp.concatenate(
                [dk_s[at + 128 : at + 256], dv_s[at + 128 : at + 256], jnp.zeros((128, 96), F32)], axis=1
            ).astype(BF)


def head_backward(core, lengths, own, oth, grad, full, top, inv):
    whole = pl.BlockSpec((8, 128, 256), lambda a: (0, 0, 0))
    line = pl.BlockSpec((1, 1, 256), lambda a: (a, 0, 0))
    out = jax.ShapeDtypeStruct((8, 128, 256), BF)
    return pl.pallas_call(
        backward_kernel,
        grid=(4,),
        in_specs=[
            pl.BlockSpec(memory_space=pltpu.SMEM),
            pl.BlockSpec(memory_space=pltpu.SMEM),
            whole,
            whole,
            pl.BlockSpec((2, HEAD_DIM, 128), lambda a: (a, 0, 0)),
            pl.BlockSpec((1, HEAD_DIM, 256), lambda a: (a, 0, 0)),
            line,
            line,
        ],
        out_specs=(whole, whole),
        out_shape=(out, out),
        scratch_shapes=[
            pltpu.VMEM((2048, HEAD_DIM), BF),
            pltpu.VMEM((2048, HEAD_DIM), BF),
            pltpu.VMEM((4, 256, HEAD_DIM), BF),
            pltpu.VMEM((2048, HEAD_DIM), F32),
            pltpu.VMEM((2048, HEAD_DIM), F32),
            pltpu.VMEM((4, 256, HEAD_DIM), F32),
        ],
        name="head_backward",
    )(core, lengths, own, oth, grad, full, top, inv)


def image_kernel(in_ref, cot_ref, gain_ref, row_ref, out_ref):
    total = jnp.zeros((32, 1), F32)
    for b in range(4):
        block = (in_ref[b].astype(F32) + in_ref[4 + b].astype(F32)) + (in_ref[8 + b].astype(F32) + in_ref[12 + b].astype(F32))
        block = block.astype(BF)
        for n in range(4):
            at = (4 * n + b) * 256
            row_ref[:, at : at + 256] = block[:, n * 256 : (n + 1) * 256]
        block = block.astype(F32)
        total = total + jnp.sum(block * block, axis=1, keepdims=True)
    inv = lax.rsqrt(total * (1.0 / 4096) + EPS)
    scaled = row_ref[...].astype(F32) * inv
    raised = cot_ref[...] * gain_ref[...]
    mean = jnp.sum(raised * scaled, axis=1, keepdims=True) * (1.0 / 4096)
    grad = (inv * (raised - scaled * mean)).astype(BF)
    for b in range(4):
        for n in range(4):
            at = (4 * n + b) * 256
            piece = grad[:, at : at + 256]
            for a in range(4):
                out_ref[4 * a + b, :, n * 256 : (n + 1) * 256] = piece


def image_rows(arrived, cotangent, gain):
    return pl.pallas_call(
        image_kernel,
        out_shape=(jax.ShapeDtypeStruct((32, 4096), BF), jax.ShapeDtypeStruct((16, 32, 1024), BF)),
        name="image_rows",
    )(arrived, cotangent, gain)


def token_kernel(text_ref, row_ref, spread_ref, cot_ref, gain_ref, out_ref, part_ref):
    spread = spread_ref[...]
    is_image = jnp.sum(spread.astype(F32), axis=1, keepdims=True) > 0.5

    def fill(k, total):
        at = pl.ds(pl.multiple_of(k * 512, 512), 512)
        rows = dotf(spread, row_ref[:, at], ((1,), (0,)))
        stream = jnp.where(is_image, rows, text_ref[:, at].astype(F32))
        out_ref[:, at] = stream.astype(BF)
        return total + jnp.sum(stream * stream, axis=1, keepdims=True)

    total = lax.fori_loop(0, 8, fill, jnp.zeros((128, 1), F32))
    inv = lax.rsqrt(total * (1.0 / 4096) + EPS)

    def scale(k, carry):
        at = pl.ds(pl.multiple_of(k * 512, 512), 512)
        scaled = out_ref[:, at].astype(F32) * inv
        part_ref[:, at] = jnp.sum(cot_ref[:, at].astype(F32) * scaled, axis=0, keepdims=True)
        out_ref[:, at] = (scaled * gain_ref[:, at]).astype(BF)
        return carry

    lax.fori_loop(0, 8, scale, 0)


def token_rows(text, rows, spread, cotangent, gain):
    return pl.pallas_call(
        token_kernel,
        out_shape=(jax.ShapeDtypeStruct((128, 4096), BF), jax.ShapeDtypeStruct((1, 4096), F32)),
        name="token_rows",
    )(text, rows, spread, cotangent, gain)


def by_half(x):
    inside = x.shape[2:]
    return jnp.moveaxis(x.reshape(8, 2, 16, *inside), 1, 0).reshape(256, *inside)


def slots_of(block):
    pair = block[:, :32, 240:242].astype(F32)
    return by_half(pair[:, :, 0] * 128.0 + pair[:, :, 1]).astype(jnp.int32)


def program(
    patch_rows,
    query,
    key_rows,
    value_rows,
    image_lengths,
    token_slots,
    out_proj,
    merge_gain,
    merger_weight,
    text_rows,
    norm_gain,
    out_grad,
):
    core = lax.axis_index(CORE)
    low_x = lax.axis_index("fsdp_1") % 2
    place = lax.axis_index(FSDP)

    pack, rows_out = packed(query[0], key_rows[0], value_rows[0], patch_rows[0], token_slots, out_proj)
    own = exchanged(pack, CHIPS)
    oth = other_core(own)
    where = jnp.stack([lax.axis_index(n) for n in EVERY]).astype(jnp.int32)
    weight = gathered_weight(merger_weight, where)
    rows_own = exchanged(rows_out, CHIPS)
    rows_oth = other_core(rows_own)

    core_scalar = core.astype(jnp.int32)[None]
    att_out, att_full, top, inv = head_forward(core_scalar, image_lengths, own, oth)
    att_own = exchanged(att_out, CHIPS).reshape(640, 256)
    att_oth = other_core(att_own)

    slots_all = jnp.concatenate([slots_of(own), slots_of(oth)], axis=0)
    rank = jnp.sum((slots_all[None, :] < slots_all[:, None]).astype(jnp.int32), axis=1)
    order = (rank[None, :] == jnp.arange(512, dtype=jnp.int32)[:, None]).astype(BF)
    normed, partial, unit, inv_std, proj = project(
        where, att_own, att_oth, rows_own, rows_oth, merge_gain[None], order, weight
    )
    arrived = exchanged(partial, FSDP)

    text = text_rows[0]
    cotangent = out_grad[0]
    token = place * 128 + jnp.arange(128, dtype=jnp.int32)
    is_image = jnp.any(slots_all[None, :] == token[:, None], axis=1)
    before = jnp.sum(
        ((slots_all[None, :] >= place * 128) & (slots_all[None, :] < token[:, None])).astype(jnp.int32), axis=1
    )
    spread = (is_image[:, None] & (before[:, None] == jnp.arange(32, dtype=jnp.int32))).astype(BF)
    image_cot = dotf(spread, cotangent, ((0,), (0,)))
    projected, image_grad = image_rows(arrived, image_cot, norm_gain[None])
    grads = exchanged(image_grad, FSDP).reshape(512, 1024)

    llm_input, norm_gain_part = token_rows(text, projected, spread, cotangent, norm_gain[None])

    back_own, back_oth = project_back(grads, order, weight)
    crossed = other_core(back_oth)
    first = back_own.astype(F32) + crossed.astype(F32)
    kept = lax.dynamic_slice_in_dim(first, low_x * 128, 128)
    sent = lax.dynamic_slice_in_dim(first, (1 - low_x) * 128, 128)
    came = other_x(sent.astype(BF))
    chunks = merger_blocks(where, normed, grads)
    merger_grad = section_sum(chunks, where[0])

    message, mine, theirs = norm_back(where, kept, came, unit, inv_std, merge_gain[None], norm_gain_part, att_own, proj)
    grad_in = exchanged(message, CHIPS)

    keep, send = head_backward(core_scalar, image_lengths, own, oth, grad_in, att_full, top, inv)
    gains = jnp.sum(grad_in[:, 240:256].astype(F32).reshape(8, 2, 8, 128), axis=(0, 1))
    summed = merged_grads(keep, other_core(send), gains)
    returned = exchanged(summed, CHIPS)
    gains = gain_rows(returned)
    gains = gains + other_core(gains)
    patch_grad, query_grad, key_grad, value_grad = unpacked(returned, grad_in)
    part = (mine.astype(F32) + other_core(theirs).astype(F32)).astype(BF).reshape(2, 4, 40, 1280)
    mine = lax.dynamic_index_in_dim(part, where[2], keepdims=False)
    theirs = lax.dynamic_index_in_dim(part, 1 - where[2], keepdims=False)
    gy = flipped(theirs, "fsdp_0", 1)
    part = (mine.astype(F32) + gy.astype(F32)).astype(BF)
    total = lax.dynamic_index_in_dim(part, where[3], keepdims=False).astype(F32)
    for far in (1, 2, 3):
        theirs = lax.dynamic_index_in_dim(part, (where[3] + far) % 4, keepdims=False)
        came_x = shifted(theirs, "fsdp_1", far)
        total = total + came_x.astype(F32)
    total = jnp.concatenate([total, gains], axis=0).astype(BF)
    total = all_sum(total, IN_SECTION)
    proj_grad = total[:40].astype(F32)
    gains = total[40:].astype(F32)
    norm_total = gains[:, 0:512].reshape(4096)
    merge_total = gains[:5, 512:768].reshape(1280)

    return (
        llm_input[None],
        patch_grad[None],
        query_grad[None],
        key_grad[None],
        value_grad[None],
        norm_total,
        merge_total,
        merger_grad,
        proj_grad,
    )


def solution(mesh):
    torus = Mesh(
        mesh.devices.reshape(2, 8, 2, 4, 2),
        ("section_0", "section_1", "fsdp_0", "fsdp_1", "fsdp_2"),
    )
    rows = P(SECTION, FSDP, None)
    placed = (
        rows,
        rows,
        rows,
        rows,
        P(SECTION, None),
        P(SECTION, FSDP),
        P(FSDP, None),
        P(),
        P(SECTION, FSDP),
        rows,
        P(),
        rows,
    )
    return jax.shard_map(
        program,
        mesh=torus,
        in_specs=placed,
        out_specs=(rows, rows, rows, rows, rows, P(), P(), P(SECTION, FSDP), P(FSDP, None)),
        check_vma=False,
    )
```
